256 devices in a mesh: gx: 4 (over z_hi), gy: 8 (over x, core), gz: 8 (over y, z_lo).
Axes of the slice: x: 4, y: 4, z: 8 (z_hi: 4, z_lo: 2; z = z_hi * 2 + z_lo), core: 2. Of those that a mesh axis runs over, the one named last changes fastest.
Arguments:
- schur: float32 [4, 8, 8, 1536, 1536], P('gx', 'gy', 'gz'), as said below
- start_block: float32 [4, 8, 8, 6, 256, 32], P('gx', 'gy', 'gz'), may hold values from -6 to 6
- resid: float32 [4, 8, 8, 1536, 128], P('gx', 'gy', 'gz'), may hold values from -6 to 6
- group_of: int32 [64], replicated, may hold values from 0 to 15, as said below
Outputs:
- correction: float32 [4, 8, 8, 1536, 128], P('gx', 'gy', 'gz')
The draws below stay inside these ranges and needn't reach their ends.
Inputs may be any that keep to these rules, and one draw needn't show every extreme that they name: Each subdomain's schur is symmetric positive definite. `group_of`: each of the 16 groups has exactly 4 subdomains.
All inputs are finite; a program needn't handle non-finite values.
Results may differ from the reference program's by a relative error of at most 0.00022.
Values sent between devices are 32-bit elements; how exact they have to be, the bound alone decides.
A program may use at most 128 MiB of HBM per device.

```python
import jax
import jax.numpy as jnp
from jax import lax

FACE = 256
NCON = 32
COLS = 128
NS_ITERS = 3
SUB_ITERS = 2
GROUP_SIZE = 4
ORDER = 1536
COARSE = 192
NSX = 4
NSY = 8
NSZ = 8
PLANE = 64
GROUPS = 16


def draw_schur(key, part):
    count = NSX * NSY * NSZ

    def single(index):
        sub_key = jax.random.fold_in(key, index)
        key_one, key_two = jax.random.split(sub_key, 2)
        normal_mat = jax.random.normal(key_one, (ORDER, ORDER), jnp.float32)
        diag_add = jax.random.uniform(key_two, (ORDER,), jnp.float32, 0.5, 1.5)
        matrix = 2.0 * jnp.dot(normal_mat, normal_mat.T, precision=lax.Precision.HIGHEST) / ORDER + jnp.diag(diag_add)
        return matrix
    return lax.map(single, jnp.arange(count)).reshape(NSX, NSY, NSZ, ORDER, ORDER)


def draw_group_of(key, part):
    shuffled = jax.random.permutation(jax.random.fold_in(key, 17), PLANE)
    return (shuffled // GROUP_SIZE).astype(jnp.int32)


def block_levels(stream_key, extent, pieces, least, largest):
    def one(position, parts):
        steps = jax.random.uniform(jax.random.fold_in(jax.random.fold_in(stream_key, 6), position), (parts,), jnp.float32, least / len(pieces), largest / len(pieces))
        return jnp.repeat(jnp.exp(steps), extent[position] // parts).reshape((-1,) + (1,) * (len(extent) - position - 1))

    loudness = one(*pieces[0])
    for cut in pieces[1:]:
        loudness = loudness * one(*cut)
    return loudness


def centred(rng, dims, deviation, most, pieces=(), kind=jnp.bfloat16):
    array = deviation * jax.random.normal(rng, dims, jnp.float32)
    if pieces:
        array = array * block_levels(rng, dims, pieces, -0.22, 0.18)
    return jnp.clip(array, -most, most).astype(kind)


def setup_inputs(seed: int = 0) -> dict:
    splits = jax.random.split(jax.random.key(seed), 5)
    schur = draw_schur(jax.random.fold_in(splits[4], 71), 0)
    start_block = centred(splits[1], (NSX, NSY, NSZ, 6, FACE, NCON), 1.0, 6.0, ((0, 4), (1, 8), (2, 8)), jnp.float32)
    resid = centred(splits[2], (NSX, NSY, NSZ, ORDER, COLS), 1.0, 6.0, ((0, 4), (1, 8), (2, 8)), jnp.float32)
    group_of = draw_group_of(jax.random.fold_in(splits[4], 71), 0)
    return {"schur": schur, "start_block": start_block, "resid": resid, "group_of": group_of}


precise = lax.Precision.HIGHEST

def neighbour_faces(stack):
    lower_x = jnp.roll(stack[:, :, :, 1], 1, axis=0)
    upper_x = jnp.roll(stack[:, :, :, 0], -1, axis=0)
    lower_y = jnp.roll(stack[:, :, :, 3], 1, axis=1)
    upper_y = jnp.roll(stack[:, :, :, 2], -1, axis=1)
    lower_z = jnp.roll(stack[:, :, :, 5], 1, axis=2)
    upper_z = jnp.roll(stack[:, :, :, 4], -1, axis=2)
    return jnp.stack([lower_x, upper_x, lower_y, upper_y, lower_z, upper_z], axis=3)

def newton_inverse(matrices):
    diag_vals = jnp.diagonal(matrices, axis1=1, axis2=2)
    identity = jnp.eye(matrices.shape[1], dtype=jnp.float32)
    inverse = identity[None] / diag_vals[:, None, :]
    for sweep in range(NS_ITERS):
        product = jnp.einsum('fij,fjk->fik', matrices, inverse, precision=precise)
        inverse = 2.0 * inverse - jnp.einsum('fij,fjk->fik', inverse, product, precision=precise)
    return inverse

def right_factor(factor, image):
    return jax.scipy.linalg.solve_triangular(factor, image.T, lower=True).T

def subspace(own, partner, inverse, starts):
    basis = starts
    for sweep in range(SUB_ITERS):
        image = jnp.einsum('fij,fjc->fic', partner, basis, precision=precise)
        image = jnp.einsum('fij,fjc->fic', inverse, image, precision=precise)
        image = jnp.einsum('fij,fjc->fic', own, image, precision=precise)
        gram = jnp.einsum('fic,fid->fcd', image, image, precision=precise)
        factor = jnp.linalg.cholesky(gram)
        basis = jax.vmap(right_factor)(factor, image)
    return basis

def local_phase(items):
    schur_one, own, partner, starts, resid_one = items
    inverse = newton_inverse(own + partner)
    basis = subspace(own, partner, inverse, starts)
    order = schur_one.shape[0]
    rows_grouped = schur_one.reshape(order, 6, FACE)
    side = jnp.einsum('igj,gjc->igc', rows_grouped, basis, precision=precise)
    side = side.reshape(6, FACE, 6, NCON)
    coarse_local = jnp.einsum('fic,figd->fcgd', basis, side, precision=precise).reshape(COARSE, COARSE)
    rhs_local = jnp.einsum('fic,fin->fcn', basis, resid_one.reshape(6, FACE, COLS), precision=precise).reshape(COARSE, COLS)
    return (inverse, basis, coarse_local, rhs_local)

def solve_one(matrix, rhs):
    factor = jnp.linalg.cholesky(matrix)
    return jax.scipy.linalg.cho_solve((factor, True), rhs)

def reference(schur, start_block, resid, group_of):
    count = NSX * NSY * NSZ
    own_all = jnp.stack([schur[:, :, :, f * FACE:(f + 1) * FACE, f * FACE:(f + 1) * FACE] for f in range(6)], axis=3)
    partner_all = neighbour_faces(own_all)
    flat = (schur.reshape(count, ORDER, ORDER), own_all.reshape(count, 6, FACE, FACE), partner_all.reshape(count, 6, FACE, FACE), start_block.reshape(count, 6, FACE, NCON), resid.reshape(count, ORDER, COLS))
    inverse, basis, coarse_local, rhs_local = lax.map(local_phase, flat)
    onehot = (group_of[:, None] == jnp.arange(GROUPS, dtype=jnp.int32)[None, :]).astype(jnp.float32)
    coarse_total = jnp.einsum('xpab,pg->xgab', coarse_local.reshape(NSX, PLANE, COARSE, COARSE), onehot, precision=precise)
    rhs_total = jnp.einsum('xpab,pg->xgab', rhs_local.reshape(NSX, PLANE, COARSE, COLS), onehot, precision=precise)
    member_matrix = coarse_total[:, group_of].reshape(count, COARSE, COARSE)
    member_rhs = rhs_total[:, group_of].reshape(count, COARSE, COLS)
    answer = jax.vmap(solve_one)(member_matrix, member_rhs)
    w_faces = jnp.einsum('dfic,dfcn->dfin', basis, answer.reshape(count, 6, NCON, COLS), precision=precise)
    own_flat = own_all.reshape(count, 6, FACE, FACE)
    products = jnp.einsum('dfij,dfjn->dfin', own_flat, w_faces, precision=precise)
    partner_y = neighbour_faces(products.reshape(NSX, NSY, NSZ, 6, FACE, COLS)).reshape(count, 6, FACE, COLS)
    correction = jnp.einsum('dfij,dfjn->dfin', inverse, products + partner_y, precision=precise)
    return correction.reshape(NSX, NSY, NSZ, ORDER, COLS)
```

```python
import functools

import jax
import jax.numpy as jnp
from jax import lax
from jax.experimental import pallas as pl
from jax.experimental.pallas import tpu as pltpu
from jax.sharding import PartitionSpec as P

FACE = 256
NCON = 32
COLS = 128
FACES = 6
ORDER = FACE * FACES
COARSE = NCON * FACES
SUB_ITERS = 2
GX, GY, GZ = 4, 8, 8
MESH = pl.DeviceIdType.MESH
NN = (((1,), (0,)), ((), ()))
NT = (((1,), (1,)), ((), ()))
F32 = jnp.float32
BF16 = jnp.bfloat16
ANY = pl.BlockSpec(memory_space=pl.ANY)
VMEM = pl.BlockSpec(memory_space=pltpu.VMEM)
SMEM = pl.BlockSpec(memory_space=pltpu.SMEM)


def here():
    return lax.axis_index("gx"), lax.axis_index("gy"), lax.axis_index("gz")


def across(face):
    gx, gy, gz = here()
    step = 1 if face % 2 else -1
    if face < 2:
        return lax.rem(gx + step + GX, GX), gy, gz
    if face < 4:
        return gx, lax.rem(gy + step + GY, GY), gz
    return gx, gy, lax.rem(gz + step + GZ, GZ)


def greet(devices):
    barrier = pltpu.get_barrier_semaphore()
    for device in devices:
        pl.semaphore_signal(barrier, inc=1, device_id=device, device_id_type=MESH)
    pl.semaphore_wait(barrier, len(devices))


def send(src, dst, send_sem, recv_sem, device):
    return pltpu.make_async_remote_copy(
        src_ref=src,
        dst_ref=dst,
        send_sem=send_sem,
        recv_sem=recv_sem,
        device_id=device,
        device_id_type=MESH,
    )


def split(value):
    high = value.astype(BF16)
    return high, (value - high.astype(F32)).astype(BF16)


def product(left, right, dims=NN):
    (left_high, left_low), (right_high, right_low) = left, right
    rows = left_high.shape[0]
    both = lax.dot_general(
        jnp.concatenate([left_high, left_low], axis=0),
        right_high,
        dims,
        preferred_element_type=F32,
    )
    cross = lax.dot_general(left_high, right_low, dims, preferred_element_type=F32)
    return both[:rows] + (both[rows:] + cross)


def faces_kernel(schur, partner, send_sem, recv_sem):
    greet([across(f) for f in range(FACES)])
    copies = []
    for f in range(FACES):
        block = pl.ds(f * FACE, FACE)
        copy = send(
            schur.at[block, block],
            partner.at[f ^ 1],
            send_sem.at[f],
            recv_sem.at[f ^ 1],
            across(f),
        )
        copy.start()
        copies.append(copy)
    for copy in copies:
        copy.wait()


def lane(value, index):
    return jnp.broadcast_to(value[:, index : index + 1], value.shape)


def local_kernel(
    schur_hbm, partner, start, resid, item, basis_out, inverse_out, side_out,
    schur, own_high, own_low, part_high, part_low, x_high, x_low, rows, image, lower, wide,
    load_sem,
):
    loads = []
    for f in range(FACES):
        block = pl.ds(f * FACE, FACE)
        copy = pltpu.make_async_copy(schur_hbm.at[block, :], schur.at[block, :], load_sem.at[f])
        copy.start()
        loads.append(copy)
    for copy in loads:
        copy.wait()
    row_ids = lax.broadcasted_iota(jnp.int32, (FACE, FACE), 0)
    col_ids = lax.broadcasted_iota(jnp.int32, (FACE, FACE), 1)

    def invert(f):
        block = pl.ds(pl.multiple_of(f * FACE, FACE), FACE)
        own = schur[block, block]
        other = partner[f]
        own_high[f], own_low[f] = split(own)
        part_high[f], part_low[f] = split(other)
        total = own + other
        diagonal = jnp.where(row_ids == col_ids, total, 0.0)
        across_row = 1.0 / jnp.sum(diagonal, axis=0, keepdims=True)
        down_col = 1.0 / jnp.sum(diagonal, axis=1, keepdims=True)
        total_parts = split(total)
        x = jnp.where(row_ids == col_ids, 2.0 * across_row, 0.0) - total * across_row * down_col
        for _ in range(2):
            x_parts = split(x)
            x = 2.0 * x - product(x_parts, split(product(total_parts, x_parts)))
        inverse_out[f] = x
        x_high[f], x_low[f] = split(x)

    def invert_pair(axis, carry):
        invert(2 * axis)
        invert(2 * axis + 1)
        return carry

    lax.fori_loop(0, 3, invert_pair, 0)
    for f in range(FACES):
        basis_out[f] = start[f].T
    rows[...] = jnp.zeros_like(rows)
    small_row = lax.broadcasted_iota(jnp.int32, (NCON, 2 * NCON), 0)
    small_col = lax.broadcasted_iota(jnp.int32, (NCON, 2 * NCON), 1)
    identity = jnp.where(small_row == small_col, 1.0, 0.0)

    def iterate(_, carry):
        for f in range(FACES):
            value = product(split(basis_out[f]), (part_high[f], part_low[f]))
            value = product(split(value), (x_high[f], x_low[f]))
            value = product(split(value), (own_high[f], own_low[f]))
            image[f] = value
            high, low = split(value)
            blank = jnp.zeros_like(high)
            shifted = (
                jnp.concatenate([blank, high], axis=0),
                jnp.concatenate([blank, low], axis=0),
            )
            gram = product((high, low), shifted, NT) + identity
            rows[pl.ds(f, NCON, stride=8), 0 : 2 * NCON] = gram
        work = [rows[8 * i : 8 * i + 8, :] for i in range(NCON)]
        for j in range(NCON):
            pivot = lane(work[j], NCON + j)
            scaled = work[j] * (1.0 / pivot)
            for i in range(j + 1, NCON):
                work[i] = work[i] - lane(work[j], NCON + i) * scaled
            rows[8 * j : 8 * j + 8, :] = work[j] * lax.rsqrt(pivot)
        for f in range(FACES):
            factor = rows[pl.ds(f, NCON, stride=8), 0:NCON]
            basis_out[f] = product(split(factor), split(image[f]))
        return carry

    lax.fori_loop(0, SUB_ITERS, iterate, 0)

    wide[...] = jnp.zeros_like(wide)
    for f in range(FACES):
        wide[f * NCON : (f + 1) * NCON, f * FACE : (f + 1) * FACE] = basis_out[f]

    def coarse_rows(f, carry):
        parts = split(basis_out[f])
        block = pl.ds(pl.multiple_of(f * FACE, FACE), FACE)
        out = pl.ds(pl.multiple_of(f * NCON, NCON), NCON)
        for g in range(FACES):
            lower[out, g * FACE : (g + 1) * FACE] = product(
                parts, split(schur[block, g * FACE : (g + 1) * FACE])
            )
        item[1, out, :] = product(parts, split(resid[block, :]))
        side = product(parts, (own_high[f], own_low[f]))
        side_out[f] = product(split(side), (x_high[f], x_low[f]))
        return carry

    lax.fori_loop(0, FACES, coarse_rows, 0)
    coarse = product(split(lower[...]), split(wide[...]), NT)
    item[0, 0:64, 0:64] = coarse[0:64, 0:64]
    item[0, 0:64, 64:128] = coarse[128:192, 128:192]
    item[0, 64:192, :] = coarse[64:192, 0:128]


def gather_kernel(
    group_of, item, basis, total, partner_basis,
    held, partial, arrived, passed, send_sem, recv_sem, basis_send, basis_recv,
):
    gx, gy, gz = here()
    x, core = gy // 2, lax.rem(gy, 2)
    y, z = gz // 2, lax.rem(gz, 2)
    kind = core

    def ring(step):
        nx = lax.rem(x + (1 - core) * step, 4)
        ny = lax.rem(y + core * step, 4)
        return gx, 2 * nx + core, 2 * ny + z

    def other_ring(step):
        nx = lax.rem(x + core * step, 4)
        ny = lax.rem(y + (1 - core) * step, 4)
        return gx, 2 * nx + core, 2 * ny + z

    mate = (gx, 2 * x + (1 - core), gz)
    over = (gx, gy, 2 * y + (1 - z))
    targets = [mate, over] + [ring(s) for s in (1, 3)] + [other_ring(s) for s in (1, 2, 3)]
    greet(targets + [across(f) for f in range(FACES)])

    half = COARSE // 2
    counter = [0]

    def copy(src, dst, device):
        n = counter[0]
        counter[0] += 1
        return send(src, dst, send_sem.at[n], recv_sem.at[n], device)

    swap = copy(item.at[1 - kind], held.at[0, 0, 1], mate)
    swap.start()
    own_over = copy(item.at[kind], held.at[0, 1, 0], over)
    own_over.start()
    pending = [swap, own_over]
    first = {}

    def spread(src, zz, cc):
        up = copy(src, held.at[1, zz, cc], ring(1))
        up.start()
        down = copy(src, held.at[3, zz, cc], ring(3))
        down.start()
        first[zz, cc] = (up, down)

    def relay(zz, cc):
        up, down = first[zz, cc]
        up.wait_recv()
        low = copy(
            held.at[1, zz, cc, pl.ds(0, half), :], held.at[2, zz, cc, pl.ds(0, half), :], ring(1)
        )
        low.start()
        down.wait_recv()
        high = copy(
            held.at[3, zz, cc, pl.ds(half, half), :], held.at[2, zz, cc, pl.ds(half, half), :],
            ring(3),
        )
        high.start()
        pending.extend([low, high])

    spread(item.at[kind], 0, 0)
    swap.wait_recv()
    mate_over = copy(held.at[0, 0, 1], held.at[0, 1, 1], over)
    mate_over.start()
    pending.append(mate_over)
    spread(held.at[0, 0, 1], 0, 1)
    basis_copies = []
    for f in range(FACES):
        c = send(basis.at[f], partner_basis.at[f ^ 1], basis_send.at[f], basis_recv.at[f ^ 1], across(f))
        c.start()
        basis_copies.append(c)
    own_over.wait_recv()
    spread(held.at[0, 1, 0], 1, 0)
    mate_over.wait_recv()
    spread(held.at[0, 1, 1], 1, 1)
    relay(0, 0)
    relay(0, 1)
    relay(1, 0)
    relay(1, 1)
    for c in pending[3:]:
        c.wait_recv()
    for c in pending:
        c.wait_send()
    for up, down in first.values():
        up.wait_send()
        down.wait_send()

    def group_at(place, cc, flip=0):
        _, gy_at, gz_at = place
        gy_at = gy_at + cc * (1 - 2 * core)
        gz_at = gz_at + flip * (1 - 2 * z)
        return group_of[gy_at * GZ + gz_at]

    sources = [
        (ring((4 - s // 4) % 4), s % 2, (s // 2) % 2) for s in range(16)
    ]
    out_copies = []
    for step in (1, 2, 3, 0):
        for cc in (0, 1):
            goal = group_at(other_ring(step), cc)
            coefs = [jnp.where(group_at(*s) == goal, 1.0, 0.0) for s in sources]

            def add_rows(r, carry):
                block = pl.ds(pl.multiple_of(r * 16, 16), 16)
                acc = None
                for s in range(16):
                    if s == 0:
                        piece = item[kind, block, :]
                    else:
                        piece = held[s // 4, (s // 2) % 2, s % 2, block, :]
                    term = coefs[s] * piece
                    acc = term if acc is None else acc + term
                partial[step, cc, block, :] = acc
                return carry

            lax.fori_loop(0, COARSE // 16, add_rows, 0)
        if step:
            c = copy(partial.at[step], arrived.at[step - 1], other_ring(step))
            c.start()
            out_copies.append(c)
    for c in out_copies:
        c.wait_recv()
    passed[...] = partial[0, 1] + arrived[0, 1] + arrived[1, 1] + arrived[2, 1]
    last = copy(passed, total.at[kind], mate)
    last.start()
    mine = partial[0, 0] + arrived[0, 0] + arrived[1, 0] + arrived[2, 0]
    total[kind] = mine
    for c in out_copies:
        c.wait_send()
    last.wait()
    for c in basis_copies:
        c.wait()


def exact(left, right):
    return lax.dot_general(
        left, right, NN, precision=lax.Precision.HIGHEST, preferred_element_type=F32
    )


def solve_kernel(total, partner_basis, partner, inverse, side, answer, mixed, system, rows):
    def mix(f, carry):
        value = product(split(partner_basis[f]), split(partner[f]))
        value = product(split(value), split(inverse[f]))
        mixed[f] = jnp.concatenate([side[f], value], axis=0).T
        return carry

    lax.fori_loop(0, FACES, mix, 0)
    system[:, 0:COLS] = total[1]
    packed = total[0]
    corner = packed[0:64, 64:128]
    first = packed[0:64, 0:64]
    below = packed[64:192, 0:64]
    middle = packed[64:128, 64:128]
    last = packed[128:192, 64:128]
    system[0:64, COLS : COLS + 192] = jnp.concatenate([first, below.T], axis=1)
    system[64:192, COLS : COLS + 192] = jnp.concatenate(
        [
            below,
            jnp.concatenate([middle, last], axis=0),
            jnp.concatenate([last.T, corner], axis=0),
        ],
        axis=1,
    )
    rows[...] = jnp.zeros_like(rows)
    small_row = lax.broadcasted_iota(jnp.int32, (NCON, NCON), 0)
    small_col = lax.broadcasted_iota(jnp.int32, (NCON, NCON), 1)
    identity = jnp.where(small_row == small_col, 1.0, 0.0)
    tall = lax.broadcasted_iota(jnp.int32, (COARSE, NCON), 0)
    for k in range(FACES):
        r0 = k * NCON
        block = system[r0 : r0 + NCON, COLS + r0 : COLS + r0 + NCON]
        rows[pl.ds(0, NCON, stride=8), 0 : 2 * NCON] = jnp.concatenate([identity, block], axis=1)
        work = [rows[8 * i : 8 * i + 8, :] for i in range(NCON)]
        for j in range(NCON):
            scaled = work[j] * (1.0 / lane(work[j], NCON + j))
            for i in range(NCON):
                if i > j:
                    work[i] = work[i] - lane(work[j], NCON + i) * scaled
                elif i < j:
                    work[i] = work[i] + lane(work[j], i) * scaled
            work[j] = scaled
        for i in range(NCON):
            rows[8 * i : 8 * i + 8, :] = work[i]
        pivot_inverse = rows[pl.ds(0, NCON, stride=8), 0:NCON]
        column = system[:, COLS + r0 : COLS + r0 + NCON]
        column = jnp.where((tall >= r0) & (tall < r0 + NCON), 0.0, column)
        scaled_rows = exact(pivot_inverse, system[r0 : r0 + NCON, :])
        system[...] = system[...] - exact(column, scaled_rows)
        system[r0 : r0 + NCON, :] = scaled_rows
    answer[...] = system[:, 0:COLS].reshape(FACES, NCON, COLS)


def answers_kernel(answer, partner_answer, send_sem, recv_sem):
    greet([across(f) for f in range(FACES)])
    copies = []
    for f in range(FACES):
        copy = send(
            answer.at[f], partner_answer.at[f ^ 1], send_sem.at[f], recv_sem.at[f ^ 1], across(f)
        )
        copy.start()
        copies.append(copy)
    for copy in copies:
        copy.wait()


def final_kernel(mixed, answer, partner_answer, correction):
    for f in range(FACES):
        both = jnp.concatenate([answer[f], partner_answer[f]], axis=0)
        correction[f * FACE : (f + 1) * FACE, :] = product(split(mixed[f]), split(both))


def array(*shape):
    return jax.ShapeDtypeStruct(shape, F32)


def remote(collective_id):
    return pltpu.CompilerParams(collective_id=collective_id, has_side_effects=True)


DMA = pltpu.SemaphoreType.DMA


def per_device(schur, start_block, resid, group_of):
    matrix = schur[0, 0, 0]
    partner = pl.pallas_call(
        faces_kernel,
        out_shape=array(FACES, FACE, FACE),
        in_specs=[ANY],
        out_specs=ANY,
        scratch_shapes=[DMA((FACES,)), DMA((FACES,))],
        compiler_params=remote(0),
        name="faces",
    )(matrix)
    blocks = (FACES, FACE, FACE)
    item, basis, inverse, side = pl.pallas_call(
        local_kernel,
        out_shape=(
            array(2, COARSE, COLS),
            array(FACES, NCON, FACE),
            array(*blocks),
            array(FACES, NCON, FACE),
        ),
        in_specs=[ANY, VMEM, VMEM, VMEM],
        out_specs=(VMEM,) * 4,
        scratch_shapes=[pltpu.VMEM((ORDER, ORDER), F32)]
        + [pltpu.VMEM(blocks, BF16)] * 6
        + [
            pltpu.VMEM((8 * NCON, 128), F32),
            pltpu.VMEM((FACES, NCON, FACE), F32),
            pltpu.VMEM((COARSE, ORDER), F32),
            pltpu.VMEM((COARSE, ORDER), F32),
            DMA((FACES,)),
        ],
        name="local",
    )(matrix, partner, start_block[0, 0, 0], resid[0, 0, 0])
    total, partner_basis = pl.pallas_call(
        gather_kernel,
        out_shape=(array(2, COARSE, COLS), array(FACES, NCON, FACE)),
        in_specs=[SMEM, VMEM, VMEM],
        out_specs=(VMEM, VMEM),
        scratch_shapes=[
            pltpu.VMEM((4, 2, 2, COARSE, COLS), F32),
            pltpu.VMEM((4, 2, COARSE, COLS), F32),
            pltpu.VMEM((3, 2, COARSE, COLS), F32),
            pltpu.VMEM((COARSE, COLS), F32),
            DMA((23,)),
            DMA((23,)),
            DMA((FACES,)),
            DMA((FACES,)),
        ],
        compiler_params=remote(1),
        name="gather",
    )(group_of, item, basis)
    answer, mixed = pl.pallas_call(
        solve_kernel,
        out_shape=(array(FACES, NCON, COLS), array(FACES, FACE, 2 * NCON)),
        in_specs=[VMEM] * 5,
        out_specs=(VMEM, VMEM),
        scratch_shapes=[
            pltpu.VMEM((COARSE, 384), F32),
            pltpu.VMEM((8 * NCON, 128), F32),
        ],
        name="solve",
    )(total, partner_basis, partner, inverse, side)
    partner_answer = pl.pallas_call(
        answers_kernel,
        out_shape=array(FACES, NCON, COLS),
        in_specs=[VMEM],
        out_specs=VMEM,
        scratch_shapes=[DMA((FACES,)), DMA((FACES,))],
        compiler_params=remote(2),
        name="answers",
    )(answer)
    correction = pl.pallas_call(
        final_kernel,
        out_shape=array(ORDER, COLS),
        in_specs=[VMEM] * 3,
        out_specs=VMEM,
        name="final",
    )(mixed, answer, partner_answer)
    return correction[None, None, None]


def solution(mesh):
    in_specs = (
        P("gx", "gy", "gz", None, None),
        P("gx", "gy", "gz", None, None, None),
        P("gx", "gy", "gz", None, None),
        P(),
    )
    out_specs = P("gx", "gy", "gz", None, None)
    return jax.shard_map(
        per_device, mesh=mesh, in_specs=in_specs, out_specs=out_specs, check_vma=False
    )
```

```python
import functools

import jax
import jax.numpy as jnp
from jax import lax
from jax.experimental import pallas as pl
from jax.experimental.pallas import tpu as pltpu
from jax.sharding import PartitionSpec as P

FACE = 256
NCON = 32
COLS = 128
FACES = 6
ORDER = FACE * FACES
COARSE = NCON * FACES
SUB_ITERS = 2
GX, GY, GZ = 4, 8, 8
MESH = pl.DeviceIdType.MESH
NN = (((1,), (0,)), ((), ()))
NT = (((1,), (1,)), ((), ()))
F32 = jnp.float32
BF16 = jnp.bfloat16
ANY = pl.BlockSpec(memory_space=pl.ANY)
VMEM = pl.BlockSpec(memory_space=pltpu.VMEM)
SMEM = pl.BlockSpec(memory_space=pltpu.SMEM)


def here():
    return lax.axis_index("gx"), lax.axis_index("gy"), lax.axis_index("gz")


def across(face):
    gx, gy, gz = here()
    step = 1 if face % 2 else -1
    if face < 2:
        return lax.rem(gx + step + GX, GX), gy, gz
    if face < 4:
        return gx, lax.rem(gy + step + GY, GY), gz
    return gx, gy, lax.rem(gz + step + GZ, GZ)


def greet(devices):
    barrier = pltpu.get_barrier_semaphore()
    for device in devices:
        pl.semaphore_signal(barrier, inc=1, device_id=device, device_id_type=MESH)
    pl.semaphore_wait(barrier, len(devices))


def send(src, dst, send_sem, recv_sem, device):
    return pltpu.make_async_remote_copy(
        src_ref=src,
        dst_ref=dst,
        send_sem=send_sem,
        recv_sem=recv_sem,
        device_id=device,
        device_id_type=MESH,
    )


def split(value):
    high = value.astype(BF16)
    return high, (value - high.astype(F32)).astype(BF16)


def product(left, right, dims=NN):
    (left_high, left_low), (right_high, right_low) = left, right
    rows = left_high.shape[0]
    both = lax.dot_general(
        jnp.concatenate([left_high, left_low], axis=0),
        right_high,
        dims,
        preferred_element_type=F32,
    )
    cross = lax.dot_general(left_high, right_low, dims, preferred_element_type=F32)
    return both[:rows] + (both[rows:] + cross)


def faces_kernel(schur, partner, send_sem, recv_sem):
    greet([across(f) for f in range(FACES)])
    copies = []
    for f in range(FACES):
        block = pl.ds(f * FACE, FACE)
        copy = send(
            schur.at[block, block],
            partner.at[f ^ 1],
            send_sem.at[f],
            recv_sem.at[f ^ 1],
            across(f),
        )
        copy.start()
        copies.append(copy)
    for copy in copies:
        copy.wait()


def row_of(value, index):
    return jnp.broadcast_to(value[index : index + 1, :], value.shape)


def eliminate(systems, column_of, panel, inverse):
    sub = lax.broadcasted_iota(jnp.int32, (8, 128), 0)
    for first in range(0, NCON, panel):
        stop = first + panel
        low = 0 if inverse else first // 8
        spread = [
            {c: {v: column_of(slabs[v], c) for v in range(low, 4)} for c in range(first, stop)}
            for slabs in systems
        ]
        for j in range(first, stop):
            vj, sj = divmod(j, 8)
            for slabs, columns in zip(systems, spread):
                pivot = row_of(columns[j][vj], sj)
                invert = 1.0 / pivot
                row = row_of(slabs[vj], sj)
                scaled = row * invert
                rest = {c: row_of(columns[c][vj], sj) * invert for c in range(j + 1, stop)}
                done = scaled if inverse else row * lax.rsqrt(pivot)
                for v in range(0 if inverse else vj, 4):
                    factor = columns[j][v]
                    new = slabs[v] - factor * scaled
                    if v == vj:
                        new = jnp.where(sub == sj, done, new)
                        if not inverse and sj:
                            new = jnp.where(sub < sj, slabs[v], new)
                    slabs[v] = new
                    for c in range(j + 1, stop):
                        updated = columns[c][v] - factor * rest[c]
                        if inverse and v == vj:
                            updated = jnp.where(sub == sj, rest[c], updated)
                        columns[c][v] = updated


def local_kernel(
    schur_hbm, partner, start, resid, item, basis_out, inverse_out, side_out,
    schur, own_high, own_low, part_high, part_low, x_high, x_low, image, lower, wide,
    load_sem,
):
    loads = []
    for f in range(FACES):
        block = pl.ds(f * FACE, FACE)
        copy = pltpu.make_async_copy(schur_hbm.at[block, :], schur.at[block, :], load_sem.at[f])
        copy.start()
        loads.append(copy)
    for copy in loads:
        copy.wait()
    row_ids = lax.broadcasted_iota(jnp.int32, (FACE, FACE), 0)
    col_ids = lax.broadcasted_iota(jnp.int32, (FACE, FACE), 1)

    def invert(f):
        block = pl.ds(pl.multiple_of(f * FACE, FACE), FACE)
        own = schur[block, block]
        other = partner[f]
        own_high[f], own_low[f] = split(own)
        part_high[f], part_low[f] = split(other)
        total = own + other
        diagonal = jnp.where(row_ids == col_ids, total, 0.0)
        across_row = 1.0 / jnp.sum(diagonal, axis=0, keepdims=True)
        down_col = 1.0 / jnp.sum(diagonal, axis=1, keepdims=True)
        total_parts = split(total)
        x = jnp.where(row_ids == col_ids, 2.0 * across_row, 0.0) - total * across_row * down_col
        for _ in range(2):
            x_parts = split(x)
            x = 2.0 * x - product(x_parts, split(product(total_parts, x_parts)))
        inverse_out[f] = x
        x_high[f], x_low[f] = split(x)

    def invert_pair(axis, carry):
        invert(2 * axis)
        invert(2 * axis + 1)
        return carry

    lax.fori_loop(0, 3, invert_pair, 0)
    for f in range(FACES):
        basis_out[f] = start[f]
    lanes = lax.broadcasted_iota(jnp.int32, (NCON, 128), 1)
    down = lax.broadcasted_iota(jnp.int32, (NCON, 128), 0)
    identity = jnp.where(lax.rem(lanes, 64) == down, 1.0, 0.0)
    left_lanes = jnp.where(lanes < NCON, 1.0, 0.0)
    right_lanes = jnp.where((lanes >= 64) & (lanes < 64 + NCON), 1.0, 0.0)
    half_base = 64 * (lax.broadcasted_iota(jnp.int32, (8, 128), 1) // 64)
    blank = jnp.zeros((NCON, FACE), BF16)

    def column_of(slab, c):
        return jnp.take_along_axis(slab, half_base + (NCON + c), axis=1)

    def iterate(_, carry):
        systems = []
        for f in range(FACES):
            value = product(split(basis_out[f]), (part_high[f], part_low[f]))
            value = product(split(value), (x_high[f], x_low[f]))
            value = product(split(value), (own_high[f], own_low[f]))
            image[f] = value
        for f in range(0, FACES, 2):
            one, two = split(image[f]), split(image[f + 1])
            gram = product(
                one, [jnp.concatenate([blank, part, blank, blank], axis=0) for part in one], NT
            )
            gram = gram + product(
                two, [jnp.concatenate([blank, blank, blank, part], axis=0) for part in two], NT
            )
            gram = gram + identity
            systems.append([gram[8 * v : 8 * v + 8] for v in range(4)])
        eliminate(systems, column_of, 4, False)
        for f in range(0, FACES, 2):
            factor = jnp.concatenate(systems[f // 2], axis=0)
            factor = jnp.concatenate([factor * left_lanes, factor * right_lanes], axis=0)
            one, two = split(image[f]), split(image[f + 1])
            both = product(
                split(factor),
                [jnp.concatenate([p, blank, q, blank], axis=0) for p, q in zip(one, two)],
            )
            basis_out[f] = both[:NCON]
            basis_out[f + 1] = both[NCON:]
        return carry

    lax.fori_loop(0, SUB_ITERS, iterate, 0)

    wide[...] = jnp.zeros_like(wide)
    for f in range(FACES):
        wide[f * NCON : (f + 1) * NCON, f * FACE : (f + 1) * FACE] = basis_out[f]

    lower[...] = jnp.zeros_like(lower)
    for f in range(FACES):
        parts = split(basis_out[f])
        block = slice(f * FACE, (f + 1) * FACE)
        out = slice(f * NCON, (f + 1) * NCON)
        for g in range(f):
            lower[out, g * FACE : (g + 1) * FACE] = product(
                parts, split(schur[block, g * FACE : (g + 1) * FACE])
            )
        side = product(parts, (own_high[f], own_low[f]))
        lower[out, block] = side
        item[1, out, :] = product(parts, split(resid[block, :]))
        side_out[f] = product(split(side), (x_high[f], x_low[f]))
    coarse = product(split(lower[...]), split(wide[...]), NT)
    item[0, 0:64, 0:64] = coarse[0:64, 0:64]
    item[0, 0:64, 64:128] = coarse[128:192, 128:192]
    item[0, 64:192, :] = coarse[64:192, 0:128]


def back_kernel(
    group_of, item, basis, partner, inverse, side, answer, mixed, partner_answer,
    held, partial, relayed, arrived, passed, total, partner_basis, system,
    send_sem, recv_sem, basis_send, basis_recv, answer_send, answer_recv,
):
    gx, gy, gz = here()
    x, core = gy // 2, lax.rem(gy, 2)
    y, z = gz // 2, lax.rem(gz, 2)
    kind = core

    def ring(step):
        nx = lax.rem(x + (1 - core) * step, 4)
        ny = lax.rem(y + core * step, 4)
        return gx, 2 * nx + core, 2 * ny + z

    def other_ring(step):
        nx = lax.rem(x + core * step, 4)
        ny = lax.rem(y + (1 - core) * step, 4)
        return gx, 2 * nx + core, 2 * ny + z

    mate = (gx, 2 * x + (1 - core), gz)
    over = (gx, gy, 2 * y + (1 - z))
    targets = [mate, over] + [ring(s) for s in (1, 3)] + [other_ring(s) for s in (1, 3)]
    greet(targets + [across(f) for f in range(FACES)])

    half = COARSE // 2
    counter = [0]

    def copy(src, dst, device):
        n = counter[0]
        counter[0] += 1
        started = send(src, dst, send_sem.at[n], recv_sem.at[n], device)
        started.start()
        return started

    def slot(step, zz, cc):
        return held.at[4 * step + 2 * zz + cc]

    swap = copy(item.at[1 - kind], slot(0, 0, 1), mate)
    own_over = copy(item.at[kind], slot(0, 1, 0), over)
    pending = [swap, own_over]
    first = {}

    def spread(src, zz, cc):
        first[zz, cc] = (
            copy(src, slot(1, zz, cc), ring(1)),
            copy(src, slot(3, zz, cc), ring(3)),
        )

    def relay(zz, cc):
        up, down = first[zz, cc]
        top, bottom = pl.ds(0, half), pl.ds(half, half)
        up.wait_recv()
        pending.append(
            copy(slot(1, zz, cc).at[top, :], slot(2, zz, cc).at[top, :], ring(1))
        )
        down.wait_recv()
        pending.append(
            copy(slot(3, zz, cc).at[bottom, :], slot(2, zz, cc).at[bottom, :], ring(3))
        )

    spread(item.at[kind], 0, 0)
    swap.wait_recv()
    mate_over = copy(slot(0, 0, 1), slot(0, 1, 1), over)
    pending.append(mate_over)
    spread(slot(0, 0, 1), 0, 1)
    basis_copies = []
    for f in range(FACES):
        c = send(
            basis.at[f], partner_basis.at[f ^ 1], basis_send.at[f], basis_recv.at[f ^ 1], across(f)
        )
        c.start()
        basis_copies.append(c)

    held[0] = item[kind]
    held[16] = jnp.zeros((COARSE, COLS), F32)

    def group_at(place, cc, flip=0):
        _, gy_at, gz_at = place
        gy_at = gy_at + cc * (1 - 2 * core)
        gz_at = gz_at + flip * (1 - 2 * z)
        return group_of[gy_at * GZ + gz_at]

    source_groups = [
        group_at(ring((4 - s // 4) % 4), s % 2, (s // 2) % 2) for s in range(16)
    ]
    members = {}
    for step in range(4):
        for cc in (0, 1):
            goal = group_at(other_ring(step), cc)
            slots = [jnp.int32(16)] * 4
            for s in range(16):
                hit = source_groups[s] == goal
                slots = [
                    jnp.where(hit, new, old)
                    for new, old in zip([jnp.int32(s)] + slots[:3], slots)
                ]
            members[step, cc] = slots

    own_over.wait_recv()
    spread(slot(0, 1, 0), 1, 0)
    mate_over.wait_recv()
    spread(slot(0, 1, 1), 1, 1)
    relay(0, 0)
    relay(0, 1)
    relay(1, 0)
    relay(1, 1)
    for c in pending[3:]:
        c.wait_recv()

    def gather_members(step):
        for cc in (0, 1):
            slots = members[step, cc]

            def add_rows(r, carry):
                block = pl.ds(pl.multiple_of(r * 32, 32), 32)
                low = held[slots[0], block, :] + held[slots[1], block, :]
                high = held[slots[2], block, :] + held[slots[3], block, :]
                partial[step, cc, block, :] = low + high
                return carry

            lax.fori_loop(0, COARSE // 32, add_rows, 0)

    top, bottom = pl.ds(0, half), pl.ds(half, half)
    gather_members(2)
    relay_up = copy(partial.at[2, :, top, :], relayed.at[0], other_ring(1))
    relay_down = copy(partial.at[2, :, bottom, :], relayed.at[1], other_ring(3))
    gather_members(1)
    up_two = copy(partial.at[1, :, bottom, :], arrived.at[0, :, bottom, :], other_ring(1))
    gather_members(3)
    down_two = copy(partial.at[3, :, top, :], arrived.at[1, :, top, :], other_ring(3))
    relay_up.wait_recv()
    partial[1, :, top, :] = partial[1, :, top, :] + relayed[0]
    up_one = copy(partial.at[1, :, top, :], arrived.at[0, :, top, :], other_ring(1))
    relay_down.wait_recv()
    partial[3, :, bottom, :] = partial[3, :, bottom, :] + relayed[1]
    down_one = copy(partial.at[3, :, bottom, :], arrived.at[1, :, bottom, :], other_ring(3))
    gather_members(0)
    sends = [relay_up, relay_down, up_two, down_two, up_one, down_one]
    for c in sends[2:]:
        c.wait_recv()
    passed[...] = partial[0, 1] + arrived[0, 1] + arrived[1, 1]
    last = copy(passed, total.at[kind], mate)
    total[kind] = partial[0, 0] + arrived[0, 0] + arrived[1, 0]
    for c in pending + sends:
        c.wait_send()
    for up, down in first.values():
        up.wait_send()
        down.wait_send()
    for c in basis_copies:
        c.wait()

    def mix(f, carry):
        value = product(split(partner_basis[f]), split(partner[f]))
        value = product(split(value), split(inverse[f]))
        mixed[f] = jnp.concatenate([side[f], value], axis=0).T
        return carry

    lax.fori_loop(0, FACES, mix, 0)
    last.wait()

    system[:, 0:COLS] = total[1]
    packed = total[0]
    row64 = lax.broadcasted_iota(jnp.int32, (64, 64), 0) // NCON
    col64 = lax.broadcasted_iota(jnp.int32, (64, 64), 1) // NCON

    def fill(block):
        return block + jnp.where(row64 > col64, block, 0.0).T

    one = packed[0:64, 0:64]
    below = packed[64:192, 0:64]
    middle = packed[64:128, 64:128]
    final = packed[128:192, 64:128]
    corner = packed[0:64, 64:128]
    blank = jnp.zeros((64, 64), F32)
    system[0:64, COLS : COLS + 256] = jnp.concatenate([fill(one), below.T, blank], axis=1)
    system[64:192, COLS : COLS + 256] = jnp.concatenate(
        [
            below,
            jnp.concatenate([fill(middle), final], axis=0),
            jnp.concatenate([final.T, fill(corner)], axis=0),
            jnp.zeros((128, 64), F32),
        ],
        axis=1,
    )
    lanes = lax.broadcasted_iota(jnp.int32, (NCON, 128), 1)
    down = lax.broadcasted_iota(jnp.int32, (NCON, 128), 0)
    tall_lane = lax.broadcasted_iota(jnp.int32, (COARSE, 128), 1)
    tall_row = lax.broadcasted_iota(jnp.int32, (COARSE, 128), 0)

    def placed(block, offset):
        parts = []
        if offset:
            parts.append(jnp.zeros((offset, block.shape[1]), block.dtype))
        parts.append(block)
        if offset + NCON < 128:
            parts.append(jnp.zeros((128 - NCON - offset, block.shape[1]), block.dtype))
        return jnp.concatenate(parts, axis=0)

    for k in range(FACES):
        rows = slice(k * NCON, (k + 1) * NCON)
        tile = slice(COLS + 128 * (k // 4), COLS + 128 * (k // 4) + 128)
        place = (k % 4) * NCON
        unit = (place + NCON) % 128
        in_unit = (lanes >= unit) & (lanes < unit + NCON)
        in_place = (lanes >= place) & (lanes < place + NCON)
        block = jnp.where(in_place, system[rows, tile], 0.0)
        block = jnp.where(lanes == down + unit, 1.0, block)
        slabs = [block[8 * v : 8 * v + 8] for v in range(4)]
        eliminate(
            [slabs],
            lambda slab, c, place=place: jnp.broadcast_to(
                slab[:, place + c : place + c + 1], slab.shape
            ),
            8,
            True,
        )
        pivot_inverse = jnp.where(in_unit, jnp.concatenate(slabs, axis=0), 0.0)
        scaled = product(
            split(pivot_inverse), [placed(part, unit) for part in split(system[rows, :])]
        )
        column = jnp.where(
            (tall_lane >= place)
            & (tall_lane < place + NCON)
            & ((tall_row < k * NCON) | (tall_row >= (k + 1) * NCON)),
            system[:, tile],
            0.0,
        )
        update = product(split(column), [placed(part, place) for part in split(scaled)])
        system[...] = system[...] - update
        system[rows, :] = scaled
    answer[...] = system[:, 0:COLS].reshape(FACES, NCON, COLS)
    copies = []
    for f in range(FACES):
        c = send(
            answer.at[f], partner_answer.at[f ^ 1], answer_send.at[f], answer_recv.at[f ^ 1],
            across(f),
        )
        c.start()
        copies.append(c)
    for c in copies:
        c.wait()


def final_kernel(mixed, answer, partner_answer, correction):
    for f in range(FACES):
        both = jnp.concatenate([answer[f], partner_answer[f]], axis=0)
        correction[f * FACE : (f + 1) * FACE, :] = product(split(mixed[f]), split(both))


def array(*shape):
    return jax.ShapeDtypeStruct(shape, F32)


def remote(collective_id):
    return pltpu.CompilerParams(collective_id=collective_id, has_side_effects=True)


DMA = pltpu.SemaphoreType.DMA


def per_device(schur, start_block, resid, group_of):
    matrix = schur[0, 0, 0]
    partner = pl.pallas_call(
        faces_kernel,
        out_shape=array(FACES, FACE, FACE),
        in_specs=[ANY],
        out_specs=ANY,
        scratch_shapes=[DMA((FACES,)), DMA((FACES,))],
        compiler_params=remote(0),
        name="faces",
    )(matrix)
    blocks = (FACES, FACE, FACE)
    item, basis, inverse, side = pl.pallas_call(
        local_kernel,
        out_shape=(
            array(2, COARSE, COLS),
            array(FACES, NCON, FACE),
            array(*blocks),
            array(FACES, NCON, FACE),
        ),
        in_specs=[ANY, VMEM, VMEM, VMEM],
        out_specs=(VMEM,) * 4,
        scratch_shapes=[pltpu.VMEM((ORDER, ORDER), F32)]
        + [pltpu.VMEM(blocks, BF16)] * 6
        + [
            pltpu.VMEM((FACES, NCON, FACE), F32),
            pltpu.VMEM((COARSE, ORDER), F32),
            pltpu.VMEM((COARSE, ORDER), F32),
            DMA((FACES,)),
        ],
        name="local",
    )(matrix, partner, jnp.swapaxes(start_block[0, 0, 0], 1, 2), resid[0, 0, 0])
    answer, mixed, partner_answer = pl.pallas_call(
        back_kernel,
        out_shape=(
            array(FACES, NCON, COLS),
            array(FACES, FACE, 2 * NCON),
            array(FACES, NCON, COLS),
        ),
        in_specs=[SMEM] + [VMEM] * 5,
        out_specs=(VMEM,) * 3,
        scratch_shapes=[
            pltpu.VMEM((17, COARSE, COLS), F32),
            pltpu.VMEM((4, 2, COARSE, COLS), F32),
            pltpu.VMEM((2, 2, COARSE // 2, COLS), F32),
            pltpu.VMEM((2, 2, COARSE, COLS), F32),
            pltpu.VMEM((COARSE, COLS), F32),
            pltpu.VMEM((2, COARSE, COLS), F32),
            pltpu.VMEM((FACES, NCON, FACE), F32),
            pltpu.VMEM((COARSE, 384), F32),
            DMA((26,)),
            DMA((26,)),
        ]
        + [DMA((FACES,))] * 4,
        compiler_params=remote(1),
        name="back",
    )(group_of, item, basis, partner, inverse, side)
    correction = pl.pallas_call(
        final_kernel,
        out_shape=array(ORDER, COLS),
        in_specs=[VMEM] * 3,
        out_specs=VMEM,
        name="final",
    )(mixed, answer, partner_answer)
    return correction[None, None, None]


def solution(mesh):
    in_specs = (
        P("gx", "gy", "gz", None, None),
        P("gx", "gy", "gz", None, None, None),
        P("gx", "gy", "gz", None, None),
        P(),
    )
    out_specs = P("gx", "gy", "gz", None, None)
    return jax.shard_map(
        per_device, mesh=mesh, in_specs=in_specs, out_specs=out_specs, check_vma=False
    )
```

```python
import functools

import jax
import jax.numpy as jnp
from jax import lax
from jax.experimental import pallas as pl
from jax.experimental.pallas import tpu as pltpu
from jax.sharding import PartitionSpec as P

FACE = 256
NCON = 32
COLS = 128
FACES = 6
ORDER = FACE * FACES
COARSE = NCON * FACES
SUB_ITERS = 2
GX, GY, GZ = 4, 8, 8
MESH = pl.DeviceIdType.MESH
NN = (((1,), (0,)), ((), ()))
NT = (((1,), (1,)), ((), ()))
F32 = jnp.float32
BF16 = jnp.bfloat16
ANY = pl.BlockSpec(memory_space=pl.ANY)
VMEM = pl.BlockSpec(memory_space=pltpu.VMEM)
SMEM = pl.BlockSpec(memory_space=pltpu.SMEM)


def here():
    return lax.axis_index("gx"), lax.axis_index("gy"), lax.axis_index("gz")


def across(face):
    gx, gy, gz = here()
    step = 1 if face % 2 else -1
    if face < 2:
        return lax.rem(gx + step + GX, GX), gy, gz
    if face < 4:
        return gx, lax.rem(gy + step + GY, GY), gz
    return gx, gy, lax.rem(gz + step + GZ, GZ)


def greet(devices):
    barrier = pltpu.get_barrier_semaphore()
    for device in devices:
        pl.semaphore_signal(barrier, inc=1, device_id=device, device_id_type=MESH)
    pl.semaphore_wait(barrier, len(devices))


def send(src, dst, send_sem, recv_sem, device):
    return pltpu.make_async_remote_copy(
        src_ref=src,
        dst_ref=dst,
        send_sem=send_sem,
        recv_sem=recv_sem,
        device_id=device,
        device_id_type=MESH,
    )


def split(value):
    high = value.astype(BF16)
    return high, (value - high.astype(F32)).astype(BF16)


def product(left, right, dims=NN):
    (left_high, left_low), (right_high, right_low) = left, right
    rows = left_high.shape[0]
    both = lax.dot_general(
        jnp.concatenate([left_high, left_low], axis=0),
        right_high,
        dims,
        preferred_element_type=F32,
    )
    cross = lax.dot_general(left_high, right_low, dims, preferred_element_type=F32)
    return both[:rows] + (both[rows:] + cross)


def row_of(value, index):
    return jnp.broadcast_to(value[index : index + 1, :], value.shape)


def eliminate(systems, column_of, panel, inverse):
    sub = lax.broadcasted_iota(jnp.int32, (8, 128), 0)
    for first in range(0, NCON, panel):
        stop = first + panel
        low = 0 if inverse else first // 8
        spread = [
            {c: {v: column_of(slabs[v], c) for v in range(low, 4)} for c in range(first, stop)}
            for slabs in systems
        ]
        for j in range(first, stop):
            vj, sj = divmod(j, 8)
            for slabs, columns in zip(systems, spread):
                pivot = row_of(columns[j][vj], sj)
                invert = 1.0 / pivot
                row = row_of(slabs[vj], sj)
                scaled = row * invert
                rest = {c: row_of(columns[c][vj], sj) * invert for c in range(j + 1, stop)}
                done = scaled if inverse else row * lax.rsqrt(pivot)
                for v in range(0 if inverse else vj, 4):
                    factor = columns[j][v]
                    new = slabs[v] - factor * scaled
                    if v == vj:
                        new = jnp.where(sub == sj, done, new)
                        if not inverse and sj:
                            new = jnp.where(sub < sj, slabs[v], new)
                    slabs[v] = new
                    for c in range(j + 1, stop):
                        updated = columns[c][v] - factor * rest[c]
                        if inverse and v == vj:
                            updated = jnp.where(sub == sj, rest[c], updated)
                        columns[c][v] = updated


def front_kernel(
    schur_hbm, start_hbm, resid_hbm, item, mixes,
    schur, high, low, other, other_high, other_low, x_high, x_low, start, other_start, resid,
    basis, lower, wide, send_sem, recv_sem, load_sem,
):
    gx, gy, gz = here()
    core = lax.rem(gy, 2)
    turns = (core, 0, core)
    mine = [2 * a + turns[a] for a in range(3)]
    theirs = [2 * a + 1 - turns[a] for a in range(3)]

    def along(a, step):
        if a == 0:
            return lax.rem(gx + step + GX, GX), gy, gz
        if a == 1:
            return gx, lax.rem(gy + step + GY, GY), gz
        return gx, gy, lax.rem(gz + step + GZ, GZ)

    ahead = [along(a, 1 - 2 * turns[a]) for a in range(3)]
    behind = [along(a, 2 * turns[a] - 1) for a in range(3)]

    def block(f, size=FACE):
        return pl.ds(pl.multiple_of(f * size, size), size)

    loads = []

    def load(src, dst):
        copy = pltpu.make_async_copy(src, dst, load_sem.at[len(loads)])
        copy.start()
        loads.append(copy)

    for f in range(FACES):
        rows = pl.ds(f * FACE, FACE)
        load(schur_hbm.at[rows, :], schur.at[rows, :])
    load(start_hbm, start)
    load(resid_hbm, resid)
    greet(ahead + behind)

    def copy(n, src, dst, device):
        started = send(src, dst, send_sem.at[n], recv_sem.at[n], device)
        started.start()
        return started

    half = FACE // 2
    faces = {}
    for a in (0, 2, 1):
        f = theirs[a]
        corner = pl.ds(pl.multiple_of(f * FACE, FACE), half)
        bottom = pl.ds(pl.multiple_of(f * FACE + half, half), half)
        faces[a] = [
            copy(
                5 * a, schur_hbm.at[bottom, block(f)], other.at[a, pl.ds(half, half), :], ahead[a]
            ),
            copy(
                5 * a + 1,
                schur_hbm.at[corner, corner],
                other.at[a, pl.ds(0, half), pl.ds(0, half)],
                ahead[a],
            ),
            copy(5 * a + 2, start_hbm.at[f], other_start.at[a], ahead[a]),
        ]

    def divide(r, carry):
        rows = pl.ds(pl.multiple_of(r * 64, 64), 64)
        high[rows, :], low[rows, :] = split(schur[rows, :])
        return carry

    lower[...] = jnp.zeros_like(lower)
    wide[...] = jnp.zeros_like(wide)
    for f in range(FACES):
        loads[f].wait()
        lax.fori_loop(f * 4, f * 4 + 4, divide, 0)
    loads[6].wait()
    loads[7].wait()

    row_ids = lax.broadcasted_iota(jnp.int32, (FACE, FACE), 0)
    col_ids = lax.broadcasted_iota(jnp.int32, (FACE, FACE), 1)

    def invert(a):
        for c in faces[a]:
            c.wait_recv()
        other[a, 0:half, half:FACE] = other[a, half:FACE, 0:half].T
        theirs_block = other[a]
        other_high[a], other_low[a] = split(theirs_block)
        total = schur[block(mine[a]), block(mine[a])] + theirs_block
        diagonal = jnp.where(row_ids == col_ids, total, 0.0)
        across_row = 1.0 / jnp.sum(diagonal, axis=0, keepdims=True)
        down_col = 1.0 / jnp.sum(diagonal, axis=1, keepdims=True)
        total_parts = split(total)
        x = jnp.where(row_ids == col_ids, 2.0 * across_row, 0.0) - total * across_row * down_col
        for _ in range(2):
            x_parts = split(x)
            x = 2.0 * x - product(x_parts, split(product(total_parts, x_parts)))
        x_high[a], x_low[a] = split(x)

    invert(1)
    invert(2)
    invert(0)

    lanes = lax.broadcasted_iota(jnp.int32, (NCON, 128), 1)
    down = lax.broadcasted_iota(jnp.int32, (NCON, 128), 0)
    identity = jnp.where(lax.rem(lanes, 64) == down, 1.0, 0.0)
    left_lanes = jnp.where(lanes < NCON, 1.0, 0.0)
    right_lanes = jnp.where((lanes >= 64) & (lanes < 64 + NCON), 1.0, 0.0)
    half_base = 64 * (lax.broadcasted_iota(jnp.int32, (8, 128), 1) // 64)
    blank = jnp.zeros((NCON, FACE), BF16)

    def column_of(slab, c):
        return jnp.take_along_axis(slab, half_base + (NCON + c), axis=1)

    def own_parts(a):
        return high[block(mine[a]), block(mine[a])], low[block(mine[a]), block(mine[a])]

    def other_parts(a):
        return other_high[a], other_low[a]

    def x_parts_of(a):
        return x_high[a], x_low[a]

    def refine(bases):
        systems, images = [], []
        for a in range(3):
            one, two = bases[a]
            both = jnp.concatenate(
                [product(split(one), other_parts(a)), product(split(two), own_parts(a))], axis=0
            )
            both = product(split(both), x_parts_of(a))
            one = split(product(split(both[:NCON]), own_parts(a)))
            two = split(product(split(both[NCON:]), other_parts(a)))
            gram = product(
                one, [jnp.concatenate([blank, part, blank, blank], axis=0) for part in one], NT
            )
            gram = gram + product(
                two, [jnp.concatenate([blank, blank, blank, part], axis=0) for part in two], NT
            )
            gram = gram + identity
            systems.append([gram[8 * v : 8 * v + 8] for v in range(4)])
            images.append([jnp.concatenate([p, blank, q, blank], axis=0) for p, q in zip(one, two)])
        eliminate(systems, column_of, 4, False)
        new = []
        for a in range(3):
            factor = jnp.concatenate(systems[a], axis=0)
            factor = jnp.concatenate([factor * left_lanes, factor * right_lanes], axis=0)
            both = product(split(factor), images[a])
            new.append((both[:NCON], both[NCON:]))
        return new

    bases = [(start[mine[a]], other_start[a]) for a in range(3)]
    for _ in range(SUB_ITERS):
        bases = refine(bases)
    returns = []
    for a in range(3):
        basis[mine[a]] = bases[a][0]
        basis[FACES + a] = bases[a][1]
        returns.append(copy(5 * a + 3, basis.at[FACES + a], basis.at[theirs[a]], behind[a]))

    def project(f, parts, columns):
        for g in columns:
            lower[block(f, NCON), block(g)] = product(
                parts, (high[block(f), block(g)], low[block(f), block(g)])
            )
        wide[block(f, NCON), block(f)] = basis[f]
        item[1, block(f, NCON), :] = product(parts, split(resid[block(f), :]))

    mix_copies = []
    for a in range(3):
        f = mine[a]
        parts = split(bases[a][0])
        side = product(parts, own_parts(a))
        lower[block(f, NCON), block(f)] = side
        facing = product(split(bases[a][1]), other_parts(a))
        both = product(split(jnp.concatenate([side, facing], axis=0)), x_parts_of(a))
        mixes[f] = both
        mixes[FACES + a] = jnp.concatenate([both[NCON:], both[:NCON]], axis=0)
        mix_copies.append(copy(5 * a + 4, mixes.at[FACES + a], mixes.at[theirs[a]], behind[a]))
        project(f, parts, mine[:a] + theirs)
    for a in range(3):
        returns[a].wait_recv()
        f = theirs[a]
        project(f, split(basis[f]), theirs[: a + 1])
    coarse = product(split(lower[...]), split(wide[...]), NT)
    blocks_row = lax.broadcasted_iota(jnp.int32, (COARSE, COARSE), 0) // NCON
    blocks_col = lax.broadcasted_iota(jnp.int32, (COARSE, COARSE), 1) // NCON
    coarse = coarse + jnp.where(blocks_row == blocks_col, 0.0, coarse).T
    item[0, 0:64, 0:64] = coarse[0:64, 0:64]
    item[0, 0:64, 64:128] = coarse[128:192, 128:192]
    item[0, 64:192, :] = coarse[64:192, 0:128]
    for a in range(3):
        for c in faces[a]:
            c.wait_send()
        returns[a].wait_send()
        mix_copies[a].wait()


def back_kernel(
    group_of, item, mixes, answer, mixed, partner_answer,
    held, partial, relayed, arrived, passed, total, system,
    send_sem, recv_sem, answer_send, answer_recv,
):
    gx, gy, gz = here()
    x, core = gy // 2, lax.rem(gy, 2)
    y, z = gz // 2, lax.rem(gz, 2)
    kind = core

    def ring(step):
        nx = lax.rem(x + (1 - core) * step, 4)
        ny = lax.rem(y + core * step, 4)
        return gx, 2 * nx + core, 2 * ny + z

    def other_ring(step):
        nx = lax.rem(x + core * step, 4)
        ny = lax.rem(y + (1 - core) * step, 4)
        return gx, 2 * nx + core, 2 * ny + z

    mate = (gx, 2 * x + (1 - core), gz)
    over = (gx, gy, 2 * y + (1 - z))
    targets = [mate, over] + [ring(s) for s in (1, 3)] + [other_ring(s) for s in (1, 3)]
    greet(targets + [across(f) for f in range(FACES)])

    half = COARSE // 2
    counter = [0]

    def copy(src, dst, device):
        n = counter[0]
        counter[0] += 1
        started = send(src, dst, send_sem.at[n], recv_sem.at[n], device)
        started.start()
        return started

    def slot(step, zz, cc):
        return held.at[4 * step + 2 * zz + cc]

    swap = copy(item.at[1 - kind], slot(0, 0, 1), mate)
    own_over = copy(item.at[kind], slot(0, 1, 0), over)
    pending = [swap, own_over]
    first = {}

    def spread(src, zz, cc):
        first[zz, cc] = (
            copy(src, slot(1, zz, cc), ring(1)),
            copy(src, slot(3, zz, cc), ring(3)),
        )

    def relay(zz, cc):
        up, down = first[zz, cc]
        top, bottom = pl.ds(0, half), pl.ds(half, half)
        up.wait_recv()
        pending.append(
            copy(slot(1, zz, cc).at[top, :], slot(2, zz, cc).at[top, :], ring(1))
        )
        down.wait_recv()
        pending.append(
            copy(slot(3, zz, cc).at[bottom, :], slot(2, zz, cc).at[bottom, :], ring(3))
        )

    spread(item.at[kind], 0, 0)
    swap.wait_recv()
    mate_over = copy(slot(0, 0, 1), slot(0, 1, 1), over)
    pending.append(mate_over)
    spread(slot(0, 0, 1), 0, 1)
    held[0] = item[kind]
    held[16] = jnp.zeros((COARSE, COLS), F32)

    def group_at(place, cc, flip=0):
        _, gy_at, gz_at = place
        gy_at = gy_at + cc * (1 - 2 * core)
        gz_at = gz_at + flip * (1 - 2 * z)
        return group_of[gy_at * GZ + gz_at]

    source_groups = [
        group_at(ring((4 - s // 4) % 4), s % 2, (s // 2) % 2) for s in range(16)
    ]
    members = {}
    for step in range(4):
        for cc in (0, 1):
            goal = group_at(other_ring(step), cc)
            slots = [jnp.int32(16)] * 4
            for s in range(16):
                hit = source_groups[s] == goal
                slots = [
                    jnp.where(hit, new, old)
                    for new, old in zip([jnp.int32(s)] + slots[:3], slots)
                ]
            members[step, cc] = slots

    own_over.wait_recv()
    spread(slot(0, 1, 0), 1, 0)
    mate_over.wait_recv()
    spread(slot(0, 1, 1), 1, 1)
    relay(0, 0)
    relay(0, 1)
    relay(1, 0)
    relay(1, 1)
    for c in pending[3:]:
        c.wait_recv()

    def gather_members(step):
        for cc in (0, 1):
            slots = members[step, cc]

            def add_rows(r, carry):
                block = pl.ds(pl.multiple_of(r * 32, 32), 32)
                low = held[slots[0], block, :] + held[slots[1], block, :]
                high = held[slots[2], block, :] + held[slots[3], block, :]
                partial[step, cc, block, :] = low + high
                return carry

            lax.fori_loop(0, COARSE // 32, add_rows, 0)

    top, bottom = pl.ds(0, half), pl.ds(half, half)
    gather_members(2)
    relay_up = copy(partial.at[2, :, top, :], relayed.at[0], other_ring(1))
    relay_down = copy(partial.at[2, :, bottom, :], relayed.at[1], other_ring(3))
    gather_members(1)
    up_two = copy(partial.at[1, :, bottom, :], arrived.at[0, :, bottom, :], other_ring(1))
    gather_members(3)
    down_two = copy(partial.at[3, :, top, :], arrived.at[1, :, top, :], other_ring(3))
    relay_up.wait_recv()
    partial[1, :, top, :] = partial[1, :, top, :] + relayed[0]
    up_one = copy(partial.at[1, :, top, :], arrived.at[0, :, top, :], other_ring(1))
    relay_down.wait_recv()
    partial[3, :, bottom, :] = partial[3, :, bottom, :] + relayed[1]
    down_one = copy(partial.at[3, :, bottom, :], arrived.at[1, :, bottom, :], other_ring(3))
    gather_members(0)
    sends = [relay_up, relay_down, up_two, down_two, up_one, down_one]
    for c in sends[2:]:
        c.wait_recv()
    passed[...] = partial[0, 1] + arrived[0, 1] + arrived[1, 1]
    last = copy(passed, total.at[kind], mate)
    total[kind] = partial[0, 0] + arrived[0, 0] + arrived[1, 0]
    for c in pending + sends:
        c.wait_send()
    for up, down in first.values():
        up.wait_send()
        down.wait_send()

    for f in range(FACES):
        mixed[f] = mixes[f].T
    last.wait()

    system[:, 0:COLS] = total[1]
    packed = total[0]
    one = packed[0:64, 0:64]
    below = packed[64:192, 0:64]
    middle = packed[64:128, 64:128]
    final = packed[128:192, 64:128]
    corner = packed[0:64, 64:128]
    blank = jnp.zeros((64, 64), F32)
    system[0:64, COLS : COLS + 256] = jnp.concatenate([one, below.T, blank], axis=1)
    system[64:192, COLS : COLS + 256] = jnp.concatenate(
        [
            below,
            jnp.concatenate([middle, final], axis=0),
            jnp.concatenate([final.T, corner], axis=0),
            jnp.zeros((128, 64), F32),
        ],
        axis=1,
    )
    lanes = lax.broadcasted_iota(jnp.int32, (NCON, 128), 1)
    down = lax.broadcasted_iota(jnp.int32, (NCON, 128), 0)
    tall_lane = lax.broadcasted_iota(jnp.int32, (COARSE, 128), 1)
    tall_row = lax.broadcasted_iota(jnp.int32, (COARSE, 128), 0)

    def placed(block, offset):
        parts = []
        if offset:
            parts.append(jnp.zeros((offset, block.shape[1]), block.dtype))
        parts.append(block)
        if offset + NCON < 128:
            parts.append(jnp.zeros((128 - NCON - offset, block.shape[1]), block.dtype))
        return jnp.concatenate(parts, axis=0)

    for k in range(FACES):
        rows = slice(k * NCON, (k + 1) * NCON)
        tile = slice(COLS + 128 * (k // 4), COLS + 128 * (k // 4) + 128)
        place = (k % 4) * NCON
        unit = (place + NCON) % 128
        in_unit = (lanes >= unit) & (lanes < unit + NCON)
        in_place = (lanes >= place) & (lanes < place + NCON)
        block = jnp.where(in_place, system[rows, tile], 0.0)
        block = jnp.where(lanes == down + unit, 1.0, block)
        slabs = [block[8 * v : 8 * v + 8] for v in range(4)]
        eliminate(
            [slabs],
            lambda slab, c, place=place: jnp.broadcast_to(
                slab[:, place + c : place + c + 1], slab.shape
            ),
            8,
            True,
        )
        pivot_inverse = jnp.where(in_unit, jnp.concatenate(slabs, axis=0), 0.0)
        scaled = product(
            split(pivot_inverse), [placed(part, unit) for part in split(system[rows, :])]
        )
        column = jnp.where(
            (tall_lane >= place)
            & (tall_lane < place + NCON)
            & ((tall_row < k * NCON) | (tall_row >= (k + 1) * NCON)),
            system[:, tile],
            0.0,
        )
        update = product(split(column), [placed(part, place) for part in split(scaled)])
        system[...] = system[...] - update
        system[rows, :] = scaled
    answer[...] = system[:, 0:COLS].reshape(FACES, NCON, COLS)
    copies = []
    for f in range(FACES):
        c = send(
            answer.at[f], partner_answer.at[f ^ 1], answer_send.at[f], answer_recv.at[f ^ 1],
            across(f),
        )
        c.start()
        copies.append(c)
    for c in copies:
        c.wait()


def final_kernel(mixed, answer, partner_answer, correction):
    for f in range(FACES):
        both = jnp.concatenate([answer[f], partner_answer[f]], axis=0)
        correction[f * FACE : (f + 1) * FACE, :] = product(split(mixed[f]), split(both))


def array(*shape):
    return jax.ShapeDtypeStruct(shape, F32)


def remote(collective_id):
    return pltpu.CompilerParams(collective_id=collective_id, has_side_effects=True)


DMA = pltpu.SemaphoreType.DMA


def per_device(schur, start_block, resid, group_of):
    matrix = schur[0, 0, 0]
    pairs = (3, FACE, FACE)
    item, mixes = pl.pallas_call(
        front_kernel,
        out_shape=(array(2, COARSE, COLS), array(FACES + 3, 2 * NCON, FACE)),
        in_specs=[ANY] * 3,
        out_specs=(VMEM,) * 2,
        scratch_shapes=[
            pltpu.VMEM((ORDER, ORDER), F32),
            pltpu.VMEM((ORDER, ORDER), BF16),
            pltpu.VMEM((ORDER, ORDER), BF16),
            pltpu.VMEM(pairs, F32),
            pltpu.VMEM(pairs, BF16),
            pltpu.VMEM(pairs, BF16),
            pltpu.VMEM(pairs, BF16),
            pltpu.VMEM(pairs, BF16),
            pltpu.VMEM((FACES, NCON, FACE), F32),
            pltpu.VMEM((3, NCON, FACE), F32),
            pltpu.VMEM((ORDER, COLS), F32),
            pltpu.VMEM((FACES + 3, NCON, FACE), F32),
            pltpu.VMEM((COARSE, ORDER), F32),
            pltpu.VMEM((COARSE, ORDER), F32),
            DMA((15,)),
            DMA((15,)),
            DMA((8,)),
        ],
        compiler_params=remote(0),
        name="front",
    )(matrix, jnp.swapaxes(start_block[0, 0, 0], 1, 2), resid[0, 0, 0])
    answer, mixed, partner_answer = pl.pallas_call(
        back_kernel,
        out_shape=(
            array(FACES, NCON, COLS),
            array(FACES, FACE, 2 * NCON),
            array(FACES, NCON, COLS),
        ),
        in_specs=[SMEM] + [VMEM] * 2,
        out_specs=(VMEM,) * 3,
        scratch_shapes=[
            pltpu.VMEM((17, COARSE, COLS), F32),
            pltpu.VMEM((4, 2, COARSE, COLS), F32),
            pltpu.VMEM((2, 2, COARSE // 2, COLS), F32),
            pltpu.VMEM((2, 2, COARSE, COLS), F32),
            pltpu.VMEM((COARSE, COLS), F32),
            pltpu.VMEM((2, COARSE, COLS), F32),
            pltpu.VMEM((COARSE, 384), F32),
            DMA((26,)),
            DMA((26,)),
        ]
        + [DMA((FACES,))] * 2,
        compiler_params=remote(1),
        name="back",
    )(group_of, item, mixes)
    correction = pl.pallas_call(
        final_kernel,
        out_shape=array(ORDER, COLS),
        in_specs=[VMEM] * 3,
        out_specs=VMEM,
        name="final",
    )(mixed, answer, partner_answer)
    return correction[None, None, None]


def solution(mesh):
    in_specs = (
        P("gx", "gy", "gz", None, None),
        P("gx", "gy", "gz", None, None, None),
        P("gx", "gy", "gz", None, None),
        P(),
    )
    out_specs = P("gx", "gy", "gz", None, None)
    return jax.shard_map(
        per_device, mesh=mesh, in_specs=in_specs, out_specs=out_specs, check_vma=False
    )
```

```python
import functools

import jax
import jax.numpy as jnp
from jax import lax
from jax.experimental import pallas as pl
from jax.experimental.pallas import tpu as pltpu
from jax.sharding import PartitionSpec as P

FACE = 256
NCON = 32
COLS = 128
FACES = 6
ORDER = FACE * FACES
COARSE = NCON * FACES
SUB_ITERS = 2
GX, GY, GZ = 4, 8, 8
MESH = pl.DeviceIdType.MESH
NN = (((1,), (0,)), ((), ()))
NT = (((1,), (1,)), ((), ()))
F32 = jnp.float32
BF16 = jnp.bfloat16
ANY = pl.BlockSpec(memory_space=pl.ANY)
VMEM = pl.BlockSpec(memory_space=pltpu.VMEM)
SMEM = pl.BlockSpec(memory_space=pltpu.SMEM)


def here():
    return lax.axis_index("gx"), lax.axis_index("gy"), lax.axis_index("gz")


def across(face):
    gx, gy, gz = here()
    step = 1 if face % 2 else -1
    if face < 2:
        return lax.rem(gx + step + GX, GX), gy, gz
    if face < 4:
        return gx, lax.rem(gy + step + GY, GY), gz
    return gx, gy, lax.rem(gz + step + GZ, GZ)


def send(src, dst, send_sem, recv_sem, device):
    return pltpu.make_async_remote_copy(
        src_ref=src,
        dst_ref=dst,
        send_sem=send_sem,
        recv_sem=recv_sem,
        device_id=device,
        device_id_type=MESH,
    )


def split(value):
    high = value.astype(BF16)
    return high, (value - high.astype(F32)).astype(BF16)


def product(left, right, dims=NN):
    (left_high, left_low), (right_high, right_low) = left, right
    rows = left_high.shape[0]
    both = lax.dot_general(
        jnp.concatenate([left_high, left_low], axis=0),
        right_high,
        dims,
        preferred_element_type=F32,
    )
    cross = lax.dot_general(left_high, right_low, dims, preferred_element_type=F32)
    return both[:rows] + (both[rows:] + cross)


def row_of(value, index):
    return jnp.broadcast_to(value[index : index + 1, :], value.shape)


def eliminate(systems, column_of, panel, inverse):
    sub = lax.broadcasted_iota(jnp.int32, (8, 128), 0)
    for first in range(0, NCON, panel):
        stop = first + panel
        low = 0 if inverse else first // 8
        spread = [
            {c: {v: column_of(slabs[v], c) for v in range(low, 4)} for c in range(first, stop)}
            for slabs in systems
        ]
        for j in range(first, stop):
            vj, sj = divmod(j, 8)
            for slabs, columns in zip(systems, spread):
                pivot = row_of(columns[j][vj], sj)
                invert = 1.0 / pivot
                row = row_of(slabs[vj], sj)
                scaled = row * invert
                rest = {c: row_of(columns[c][vj], sj) * invert for c in range(j + 1, stop)}
                done = scaled if inverse else row * lax.rsqrt(pivot)
                for v in range(0 if inverse else vj, 4):
                    factor = columns[j][v]
                    new = slabs[v] - factor * scaled
                    if v == vj:
                        new = jnp.where(sub == sj, done, new)
                        if not inverse and sj:
                            new = jnp.where(sub < sj, slabs[v], new)
                    slabs[v] = new
                    for c in range(j + 1, stop):
                        updated = columns[c][v] - factor * rest[c]
                        if inverse and v == vj:
                            updated = jnp.where(sub == sj, rest[c], updated)
                        columns[c][v] = updated


def main_kernel(
    group_of, schur_hbm, start_hbm, resid_hbm, correction,
    stage, packed_out, packed_in, schur, high, low, other, other_high, other_low, x_high, x_low, start, other_start, resid,
    basis, lower, wide, item, mixes, mixed_high, mixed_low,
    pieces, held, sums, got, total, system, answer, partner_answer,
    send_sem, recv_sem, load_sem,
):
    gx, gy, gz = here()
    core = lax.rem(gy, 2)
    turns = (core, 0, core)
    mine = [2 * a + turns[a] for a in range(3)]
    theirs = [2 * a + 1 - turns[a] for a in range(3)]

    def along(a, step):
        if a == 0:
            return lax.rem(gx + step + GX, GX), gy, gz
        if a == 1:
            return gx, lax.rem(gy + step + GY, GY), gz
        return gx, gy, lax.rem(gz + step + GZ, GZ)

    ahead = [along(a, 1 - 2 * turns[a]) for a in range(3)]
    behind = [along(a, 2 * turns[a] - 1) for a in range(3)]
    x = gy // 2
    y, z = gz // 2, lax.rem(gz, 2)

    def plane_device(i, cc):
        to_x, to_y, to_z = lax.rem(x + i % 4, 4), lax.rem(y + (i // 4) % 4, 4), lax.rem(z + i // 16, 2)
        to_core = core + cc * (1 - 2 * core)
        return to_core, (to_x * 4 + to_y) * 2 + to_z, (gx, 2 * to_x + to_core, 2 * to_y + to_z)

    chip = (x * 4 + y) * 2 + z
    line = gy * GZ + gz
    plane = [plane_device(i, cc) for i in range(32) for cc in range(2) if i or cc]

    def block(f, size=FACE):
        return pl.ds(pl.multiple_of(f * size, size), size)

    loads = []

    def load(src, dst):
        copy = pltpu.make_async_copy(src, dst, load_sem.at[len(loads)])
        copy.start()
        loads.append(copy)

    for a in range(3):
        load(schur_hbm.at[block(theirs[a]), block(theirs[a])], stage.at[a])
    barrier = pltpu.get_barrier_semaphore()
    greeted = [ahead[0], behind[0]] + [place for _, _, place in plane]
    for device in greeted:
        pl.semaphore_signal(barrier, inc=1, device_id=device, device_id_type=MESH)
    for f in range(FACES):
        rows = pl.ds(f * FACE, FACE)
        load(schur_hbm.at[rows, :], schur.at[rows, :])
    load(start_hbm, start)
    load(resid_hbm, resid)
    half = FACE // 2
    half_rows = lax.broadcasted_iota(jnp.int32, (half, half), 0)
    half_cols = lax.broadcasted_iota(jnp.int32, (half, half), 1)
    for a in range(3):
        loads[a].wait()
        first_block = stage[a, 0:half, 0:half]
        second_block = stage[a, half:FACE, half:FACE]
        packed_out[a, 0:half] = stage[a, half:FACE, 0:half]
        packed_out[a, half:FACE] = jnp.where(half_rows >= half_cols, first_block, second_block)
        packed_out[a, FACE : FACE + 8] = jnp.broadcast_to(
            jnp.sum(
                jnp.where(half_rows == half_cols, second_block, 0.0), axis=0, keepdims=True
            ),
            (8, half),
        )
    pl.semaphore_wait(barrier, len(greeted))
    counter = [0]

    def copy(src, dst, device):
        n = counter[0]
        counter[0] += 1
        started = send(src, dst, send_sem.at[n], recv_sem.at[n], device)
        started.start()
        return started

    faces = {a: copy(packed_out.at[a], packed_in.at[a], ahead[a]) for a in (2, 0, 1)}
    starts = [copy(start_hbm.at[theirs[a]], other_start.at[a], ahead[a]) for a in range(3)]

    def divide(r, carry):
        rows = pl.ds(pl.multiple_of(r * 64, 64), 64)
        high[rows, :], low[rows, :] = split(schur[rows, :])
        return carry

    lower[...] = jnp.zeros_like(lower)
    wide[...] = jnp.zeros_like(wide)
    for f in range(FACES):
        loads[3 + f].wait()
        lax.fori_loop(f * 4, f * 4 + 4, divide, 0)
    loads[9].wait()
    loads[10].wait()

    row_ids = lax.broadcasted_iota(jnp.int32, (FACE, FACE), 0)
    col_ids = lax.broadcasted_iota(jnp.int32, (FACE, FACE), 1)

    def invert(a):
        faces[a].wait_recv()
        below = packed_in[a, 0:half]
        folded = packed_in[a, half:FACE]
        mirrored = folded.T
        second_diagonal = jnp.broadcast_to(packed_in[a, FACE : FACE + 1], (half, half))
        other[a, half:FACE, 0:half] = below
        other[a, 0:half, half:FACE] = below.T
        other[a, 0:half, 0:half] = jnp.where(half_rows >= half_cols, folded, mirrored)
        other[a, half:FACE, half:FACE] = jnp.where(
            half_rows < half_cols,
            folded,
            jnp.where(half_rows == half_cols, second_diagonal, mirrored),
        )
        theirs_block = other[a]
        other_high[a], other_low[a] = split(theirs_block)
        total = schur[block(mine[a]), block(mine[a])] + theirs_block
        diagonal = jnp.where(row_ids == col_ids, total, 0.0)
        across_row = 1.0 / jnp.sum(diagonal, axis=0, keepdims=True)
        down_col = 1.0 / jnp.sum(diagonal, axis=1, keepdims=True)
        total_parts = split(total)
        x = jnp.where(row_ids == col_ids, 2.0 * across_row, 0.0) - total * across_row * down_col
        for _ in range(2):
            x_parts = split(x)
            x = 2.0 * x - product(x_parts, split(product(total_parts, x_parts)))
        x_high[a], x_low[a] = split(x)

    invert(1)
    invert(2)
    invert(0)

    lanes = lax.broadcasted_iota(jnp.int32, (NCON, 128), 1)
    down = lax.broadcasted_iota(jnp.int32, (NCON, 128), 0)
    identity = jnp.where(lax.rem(lanes, 64) == down, 1.0, 0.0)
    left_lanes = jnp.where(lanes < NCON, 1.0, 0.0)
    right_lanes = jnp.where((lanes >= 64) & (lanes < 64 + NCON), 1.0, 0.0)
    half_base = 64 * (lax.broadcasted_iota(jnp.int32, (8, 128), 1) // 64)
    blank = jnp.zeros((NCON, FACE), BF16)

    def column_of(slab, c):
        return jnp.take_along_axis(slab, half_base + (NCON + c), axis=1)

    def own_parts(a):
        return high[block(mine[a]), block(mine[a])], low[block(mine[a]), block(mine[a])]

    def other_parts(a):
        return other_high[a], other_low[a]

    def x_parts_of(a):
        return x_high[a], x_low[a]

    def refine(bases):
        systems, images = [], []
        for a in range(3):
            one, two = bases[a]
            both = jnp.concatenate(
                [product(split(one), other_parts(a)), product(split(two), own_parts(a))], axis=0
            )
            both = product(split(both), x_parts_of(a))
            one = split(product(split(both[:NCON]), own_parts(a)))
            two = split(product(split(both[NCON:]), other_parts(a)))
            gram = product(
                one, [jnp.concatenate([blank, part, blank, blank], axis=0) for part in one], NT
            )
            gram = gram + product(
                two, [jnp.concatenate([blank, blank, blank, part], axis=0) for part in two], NT
            )
            gram = gram + identity
            systems.append([gram[8 * v : 8 * v + 8] for v in range(4)])
            images.append([jnp.concatenate([p, blank, q, blank], axis=0) for p, q in zip(one, two)])
        eliminate(systems, column_of, 4, False)
        new = []
        for a in range(3):
            factor = jnp.concatenate(systems[a], axis=0)
            factor = jnp.concatenate([factor * left_lanes, factor * right_lanes], axis=0)
            both = product(split(factor), images[a])
            new.append((both[:NCON], both[NCON:]))
        return new

    for c in starts:
        c.wait_recv()
    bases = [(start[mine[a]], other_start[a]) for a in range(3)]
    for _ in range(SUB_ITERS):
        bases = refine(bases)
    returns = []
    for a in range(3):
        basis[mine[a]] = bases[a][0]
        basis[FACES + a] = bases[a][1]
        returns.append(copy(basis.at[FACES + a], basis.at[theirs[a]], behind[a]))

    def project(f, parts, columns):
        for g in columns:
            lower[block(f, NCON), block(g)] = product(
                parts, (high[block(f), block(g)], low[block(f), block(g)])
            )
        wide[block(f, NCON), block(f)] = basis[f]
        item[1, block(f, NCON), :] = product(parts, split(resid[block(f), :]))

    mix_copies = []
    for a in range(3):
        f = mine[a]
        parts = split(bases[a][0])
        side = product(parts, own_parts(a))
        lower[block(f, NCON), block(f)] = side
        facing = product(split(bases[a][1]), other_parts(a))
        both = product(split(jnp.concatenate([side, facing], axis=0)), x_parts_of(a))
        mixes[f] = both
        mixes[FACES + a] = jnp.concatenate([both[NCON:], both[:NCON]], axis=0)
        mix_copies.append(copy(mixes.at[FACES + a], mixes.at[theirs[a]], behind[a]))
        project(f, parts, mine[:a] + theirs)
    for a in range(3):
        returns[a].wait_recv()
        f = theirs[a]
        project(f, split(basis[f]), theirs[: a + 1])
    coarse = product(split(lower[...]), split(wide[...]), NT)
    blocks_row = lax.broadcasted_iota(jnp.int32, (COARSE, COARSE), 0) // NCON
    blocks_col = lax.broadcasted_iota(jnp.int32, (COARSE, COARSE), 1) // NCON
    coarse = coarse + jnp.where(blocks_row == blocks_col, 0.0, coarse).T
    item[0, 0:64, 0:64] = coarse[0:64, 0:64]
    item[0, 0:64, 64:128] = coarse[128:192, 128:192]
    item[0, 64:192, :] = coarse[64:192, 0:128]

    def six(ref, index):
        return ref.at[pl.ds(pl.multiple_of(index * 8, 8), 6), :]

    for k in range(2):
        for c in range(32):
            pieces[8 * (32 * k + c) : 8 * (32 * k + c) + 6, :] = item[k, 6 * c : 6 * c + 6, :]
    scattered = [
        copy(six(pieces, 32 * to_core + to_chip), six(held, line), place)
        for to_core, to_chip, place in plane
    ]
    here_six = pl.ds(pl.multiple_of(line * 8, 8), 6)
    held[here_six, :] = pieces[pl.ds(pl.multiple_of((32 * core + chip) * 8, 8), 6), :]
    groups = jnp.broadcast_to(group_of[...].astype(F32), (64, 64))
    same = jnp.where(groups == groups.T, 1.0, 0.0).astype(BF16)
    for a in range(3):
        mix_copies[a].wait_recv()
    for f in range(FACES):
        mixed_high[f], mixed_low[f] = split(mixes[f].T)
    for c in scattered:
        c.wait_recv()
    for j in range(6):
        value = held[pl.ds(j, 64, stride=8), :]
        one = value.astype(BF16)
        rest = value - one.astype(F32)
        two = rest.astype(BF16)
        three = (rest - two.astype(F32)).astype(BF16)
        added = lax.dot_general(
            same, jnp.concatenate([one, two, three], axis=1), NN, preferred_element_type=F32
        )
        sums[pl.ds(j, 64, stride=8), :] = added[:, 0:128] + (added[:, 128:256] + added[:, 256:384])
    returned = [
        copy(six(sums, place[1] * GZ + place[2]), six(got, 32 * core + chip), place)
        for _, _, place in plane
    ]
    got[pl.ds(pl.multiple_of((32 * core + chip) * 8, 8), 6), :] = sums[here_six, :]
    for c in returned:
        c.wait_recv()
    for k in range(2):
        for c in range(32):
            total[k, 6 * c : 6 * c + 6, :] = got[8 * (32 * k + c) : 8 * (32 * k + c) + 6, :]

    system[:, 0:COLS] = total[1]
    packed = total[0]
    one = packed[0:64, 0:64]
    below = packed[64:192, 0:64]
    middle = packed[64:128, 64:128]
    final = packed[128:192, 64:128]
    corner = packed[0:64, 64:128]
    blank = jnp.zeros((64, 64), F32)
    system[0:64, COLS : COLS + 256] = jnp.concatenate([one, below.T, blank], axis=1)
    system[64:192, COLS : COLS + 256] = jnp.concatenate(
        [
            below,
            jnp.concatenate([middle, final], axis=0),
            jnp.concatenate([final.T, corner], axis=0),
            jnp.zeros((128, 64), F32),
        ],
        axis=1,
    )
    lanes = lax.broadcasted_iota(jnp.int32, (NCON, 128), 1)
    down = lax.broadcasted_iota(jnp.int32, (NCON, 128), 0)
    tall_lane = lax.broadcasted_iota(jnp.int32, (COARSE, 128), 1)
    tall_row = lax.broadcasted_iota(jnp.int32, (COARSE, 128), 0)

    def placed(block, offset):
        parts = []
        if offset:
            parts.append(jnp.zeros((offset, block.shape[1]), block.dtype))
        parts.append(block)
        if offset + NCON < 128:
            parts.append(jnp.zeros((128 - NCON - offset, block.shape[1]), block.dtype))
        return jnp.concatenate(parts, axis=0)

    for k in range(FACES):
        rows = slice(k * NCON, (k + 1) * NCON)
        tile = slice(COLS + 128 * (k // 4), COLS + 128 * (k // 4) + 128)
        place = (k % 4) * NCON
        unit = (place + NCON) % 128
        in_unit = (lanes >= unit) & (lanes < unit + NCON)
        in_place = (lanes >= place) & (lanes < place + NCON)
        block = jnp.where(in_place, system[rows, tile], 0.0)
        block = jnp.where(lanes == down + unit, 1.0, block)
        slabs = [block[8 * v : 8 * v + 8] for v in range(4)]
        eliminate(
            [slabs],
            lambda slab, c, place=place: jnp.broadcast_to(
                slab[:, place + c : place + c + 1], slab.shape
            ),
            8,
            True,
        )
        pivot_inverse = jnp.where(in_unit, jnp.concatenate(slabs, axis=0), 0.0)
        scaled = product(
            split(pivot_inverse), [placed(part, unit) for part in split(system[rows, :])]
        )
        column = jnp.where(
            (tall_lane >= place)
            & (tall_lane < place + NCON)
            & ((tall_row < k * NCON) | (tall_row >= (k + 1) * NCON)),
            system[:, tile],
            0.0,
        )
        update = product(split(column), [placed(part, place) for part in split(scaled)])
        system[...] = system[...] - update
        system[rows, :] = scaled
    answer[...] = system[:, 0:COLS].reshape(FACES, NCON, COLS)
    answers = [
        copy(answer.at[f], partner_answer.at[f ^ 1], across(f)) for f in range(FACES)
    ]
    for f in (2, 3, 4, 5, 0, 1):
        answers[f ^ 1].wait_recv()
        both = jnp.concatenate([answer[f], partner_answer[f]], axis=0)
        correction[f * FACE : (f + 1) * FACE, :] = product(
            (mixed_high[f], mixed_low[f]), split(both)
        )
    for a in range(3):
        for c in (faces[a], starts[a], returns[a], mix_copies[a]):
            c.wait_send()
    for c in scattered + returned + answers:
        c.wait_send()


def array(*shape):
    return jax.ShapeDtypeStruct(shape, F32)


def remote(collective_id):
    return pltpu.CompilerParams(collective_id=collective_id, has_side_effects=True)


DMA = pltpu.SemaphoreType.DMA


def per_device(schur, start_block, resid, group_of):
    matrix = schur[0, 0, 0]
    pairs = (3, FACE, FACE)
    copies = 12 + 2 * 63 + 6
    correction = pl.pallas_call(
        main_kernel,
        out_shape=array(ORDER, COLS),
        in_specs=[VMEM] + [ANY] * 3,
        out_specs=VMEM,
        scratch_shapes=[
            pltpu.VMEM(pairs, F32),
            pltpu.VMEM((3, FACE + 8, FACE // 2), F32),
            pltpu.VMEM((3, FACE + 8, FACE // 2), F32),
            pltpu.VMEM((ORDER, ORDER), F32),
            pltpu.VMEM((ORDER, ORDER), BF16),
            pltpu.VMEM((ORDER, ORDER), BF16),
            pltpu.VMEM(pairs, F32),
            pltpu.VMEM(pairs, BF16),
            pltpu.VMEM(pairs, BF16),
            pltpu.VMEM(pairs, BF16),
            pltpu.VMEM(pairs, BF16),
            pltpu.VMEM((FACES, NCON, FACE), F32),
            pltpu.VMEM((3, NCON, FACE), F32),
            pltpu.VMEM((ORDER, COLS), F32),
            pltpu.VMEM((FACES + 3, NCON, FACE), F32),
            pltpu.VMEM((COARSE, ORDER), F32),
            pltpu.VMEM((COARSE, ORDER), F32),
            pltpu.VMEM((2, COARSE, COLS), F32),
            pltpu.VMEM((FACES + 3, 2 * NCON, FACE), F32),
            pltpu.VMEM((FACES, FACE, 2 * NCON), BF16),
            pltpu.VMEM((FACES, FACE, 2 * NCON), BF16),
            pltpu.VMEM((512, COLS), F32),
            pltpu.VMEM((512, COLS), F32),
            pltpu.VMEM((512, COLS), F32),
            pltpu.VMEM((512, COLS), F32),
            pltpu.VMEM((2, COARSE, COLS), F32),
            pltpu.VMEM((COARSE, 384), F32),
            pltpu.VMEM((FACES, NCON, COLS), F32),
            pltpu.VMEM((FACES, NCON, COLS), F32),
            DMA((copies,)),
            DMA((copies,)),
            DMA((11,)),
        ],
        compiler_params=remote(0),
        name="main",
    )(group_of[None], matrix, jnp.swapaxes(start_block[0, 0, 0], 1, 2), resid[0, 0, 0])
    return correction[None, None, None]


def solution(mesh):
    in_specs = (
        P("gx", "gy", "gz", None, None),
        P("gx", "gy", "gz", None, None, None),
        P("gx", "gy", "gz", None, None),
        P(),
    )
    out_specs = P("gx", "gy", "gz", None, None)
    return jax.shard_map(
        per_device, mesh=mesh, in_specs=in_specs, out_specs=out_specs, check_vma=False
    )
```

```python
import functools

import jax
import jax.numpy as jnp
from jax import lax
from jax.experimental import pallas as pl
from jax.experimental.pallas import tpu as pltpu
from jax.sharding import PartitionSpec as P

FACE = 256
NCON = 32
COLS = 128
FACES = 6
ORDER = FACE * FACES
COARSE = NCON * FACES
SUB_ITERS = 2
GX, GY, GZ = 4, 8, 8
MESH = pl.DeviceIdType.MESH
NN = (((1,), (0,)), ((), ()))
NT = (((1,), (1,)), ((), ()))
F32 = jnp.float32
BF16 = jnp.bfloat16
ANY = pl.BlockSpec(memory_space=pl.ANY)
VMEM = pl.BlockSpec(memory_space=pltpu.VMEM)
SMEM = pl.BlockSpec(memory_space=pltpu.SMEM)


def here():
    return lax.axis_index("gx"), lax.axis_index("gy"), lax.axis_index("gz")


def across(face):
    gx, gy, gz = here()
    step = 1 if face % 2 else -1
    if face < 2:
        return lax.rem(gx + step + GX, GX), gy, gz
    if face < 4:
        return gx, lax.rem(gy + step + GY, GY), gz
    return gx, gy, lax.rem(gz + step + GZ, GZ)


def send(src, dst, send_sem, recv_sem, device):
    return pltpu.make_async_remote_copy(
        src_ref=src,
        dst_ref=dst,
        send_sem=send_sem,
        recv_sem=recv_sem,
        device_id=device,
        device_id_type=MESH,
    )


def split(value):
    high = value.astype(BF16)
    return high, (value - high.astype(F32)).astype(BF16)


def product(left, right, dims=NN):
    (left_high, left_low), (right_high, right_low) = left, right
    rows = left_high.shape[0]
    both = lax.dot_general(
        jnp.concatenate([left_high, left_low], axis=0),
        right_high,
        dims,
        preferred_element_type=F32,
    )
    cross = lax.dot_general(left_high, right_low, dims, preferred_element_type=F32)
    return both[:rows] + (both[rows:] + cross)


def row_of(value, index):
    return jnp.broadcast_to(value[index : index + 1, :], value.shape)


def eliminate(systems, column_of, panel, inverse):
    sub = lax.broadcasted_iota(jnp.int32, (8, 128), 0)
    for first in range(0, NCON, panel):
        stop = first + panel
        low = 0 if inverse else first // 8
        spread = [
            {c: {v: column_of(slabs[v], c) for v in range(low, 4)} for c in range(first, stop)}
            for slabs in systems
        ]
        for j in range(first, stop):
            vj, sj = divmod(j, 8)
            for slabs, columns in zip(systems, spread):
                pivot = row_of(columns[j][vj], sj)
                invert = 1.0 / pivot
                row = row_of(slabs[vj], sj)
                scaled = row * invert
                rest = {c: row_of(columns[c][vj], sj) * invert for c in range(j + 1, stop)}
                done = scaled if inverse else row * lax.rsqrt(pivot)
                for v in range(0 if inverse else vj, 4):
                    factor = columns[j][v]
                    new = slabs[v] - factor * scaled
                    if v == vj:
                        new = jnp.where(sub == sj, done, new)
                        if not inverse and sj:
                            new = jnp.where(sub < sj, slabs[v], new)
                    slabs[v] = new
                    for c in range(j + 1, stop):
                        updated = columns[c][v] - factor * rest[c]
                        if inverse and v == vj:
                            updated = jnp.where(sub == sj, rest[c], updated)
                        columns[c][v] = updated


def main_kernel(
    group_of, schur_hbm, start_hbm, resid_hbm, correction,
    stage, packed_out, packed_in, schur, high, low, other, other_high, other_low, x_high, x_low, start, other_start, resid,
    basis, lower, wide, item, mixes, mixed_high, mixed_low,
    pieces, held, sums, got, total, system, answer, partner_answer,
    send_sem, recv_sem, load_sem, plane_sem,
):
    gx, gy, gz = here()
    core = lax.rem(gy, 2)
    turns = (core, 0, core)
    mine = [2 * a + turns[a] for a in range(3)]
    theirs = [2 * a + 1 - turns[a] for a in range(3)]

    def along(a, step):
        if a == 0:
            return lax.rem(gx + step + GX, GX), gy, gz
        if a == 1:
            return gx, lax.rem(gy + step + GY, GY), gz
        return gx, gy, lax.rem(gz + step + GZ, GZ)

    ahead = [along(a, 1 - 2 * turns[a]) for a in range(3)]
    behind = [along(a, 2 * turns[a] - 1) for a in range(3)]
    x = gy // 2
    y, z = gz // 2, lax.rem(gz, 2)

    def plane_device(i, cc):
        to_x, to_y, to_z = lax.rem(x + i % 4, 4), lax.rem(y + (i // 4) % 4, 4), lax.rem(z + i // 16, 2)
        to_core = core + cc * (1 - 2 * core)
        return to_core, (to_x * 4 + to_y) * 2 + to_z, (gx, 2 * to_x + to_core, 2 * to_y + to_z)

    chip = (x * 4 + y) * 2 + z
    line = gy * GZ + gz
    hops = {i: (i % 4) * (4 - i % 4) + (i // 4 % 4) * (4 - i // 4 % 4) + 3 * (i // 16) for i in range(32)}
    far_first = sorted(range(32), key=lambda i: -hops[i])
    plane = [plane_device(i, cc) for i in far_first for cc in range(2) if i or cc]

    def block(f, size=FACE):
        return pl.ds(pl.multiple_of(f * size, size), size)

    loads = []

    def load(src, dst):
        copy = pltpu.make_async_copy(src, dst, load_sem.at[len(loads)])
        copy.start()
        loads.append(copy)

    for a in range(3):
        load(schur_hbm.at[block(theirs[a]), block(theirs[a])], stage.at[a])
    barrier = pltpu.get_barrier_semaphore()
    row_devices = [(gx, lax.rem(gy + i, GY), gz) for i in range(1, GY)]
    column_devices = [(gx, gy, lax.rem(gz + i, GZ)) for i in range(1, GZ)]
    greeted = [ahead[0], behind[0]] + row_devices + column_devices
    for device in greeted:
        pl.semaphore_signal(barrier, inc=1, device_id=device, device_id_type=MESH)
    for f in range(FACES):
        rows = pl.ds(f * FACE, FACE)
        load(schur_hbm.at[rows, :], schur.at[rows, :])
    load(start_hbm, start)
    load(resid_hbm, resid)
    half = FACE // 2
    half_rows = lax.broadcasted_iota(jnp.int32, (half, half), 0)
    half_cols = lax.broadcasted_iota(jnp.int32, (half, half), 1)
    for a in range(3):
        loads[a].wait()
        first_block = stage[a, 0:half, 0:half]
        second_block = stage[a, half:FACE, half:FACE]
        packed_out[a, 0:half] = stage[a, half:FACE, 0:half]
        packed_out[a, half:FACE] = jnp.where(half_rows >= half_cols, first_block, second_block)
        packed_out[a, FACE : FACE + 8] = jnp.broadcast_to(
            jnp.sum(
                jnp.where(half_rows == half_cols, second_block, 0.0), axis=0, keepdims=True
            ),
            (8, half),
        )
    pl.semaphore_wait(barrier, len(greeted))
    for device in row_devices:
        pl.semaphore_signal(plane_sem, inc=1, device_id=device, device_id_type=MESH)
    counter = [0]

    def copy(src, dst, device):
        n = counter[0]
        counter[0] += 1
        started = send(src, dst, send_sem.at[n], recv_sem.at[n], device)
        started.start()
        return started

    faces = {a: copy(packed_out.at[a], packed_in.at[a], ahead[a]) for a in (2, 0, 1)}
    starts = [copy(start_hbm.at[theirs[a]], other_start.at[a], ahead[a]) for a in range(3)]

    def divide(r, carry):
        rows = pl.ds(pl.multiple_of(r * 64, 64), 64)
        high[rows, :], low[rows, :] = split(schur[rows, :])
        return carry

    lower[...] = jnp.zeros_like(lower)
    wide[...] = jnp.zeros_like(wide)
    for f in range(FACES):
        loads[3 + f].wait()
        lax.fori_loop(f * 4, f * 4 + 4, divide, 0)
    loads[9].wait()
    loads[10].wait()

    row_ids = lax.broadcasted_iota(jnp.int32, (FACE, FACE), 0)
    col_ids = lax.broadcasted_iota(jnp.int32, (FACE, FACE), 1)

    def invert(a):
        faces[a].wait_recv()
        below = packed_in[a, 0:half]
        folded = packed_in[a, half:FACE]
        mirrored = folded.T
        second_diagonal = jnp.broadcast_to(packed_in[a, FACE : FACE + 1], (half, half))
        other[a, half:FACE, 0:half] = below
        other[a, 0:half, half:FACE] = below.T
        other[a, 0:half, 0:half] = jnp.where(half_rows >= half_cols, folded, mirrored)
        other[a, half:FACE, half:FACE] = jnp.where(
            half_rows < half_cols,
            folded,
            jnp.where(half_rows == half_cols, second_diagonal, mirrored),
        )
        theirs_block = other[a]
        other_high[a], other_low[a] = split(theirs_block)
        total = schur[block(mine[a]), block(mine[a])] + theirs_block
        diagonal = jnp.where(row_ids == col_ids, total, 0.0)
        across_row = 1.0 / jnp.sum(diagonal, axis=0, keepdims=True)
        down_col = 1.0 / jnp.sum(diagonal, axis=1, keepdims=True)
        total_parts = split(total)
        x = jnp.where(row_ids == col_ids, 2.0 * across_row, 0.0) - total * across_row * down_col
        for _ in range(2):
            x_parts = split(x)
            x = 2.0 * x - product(x_parts, split(product(total_parts, x_parts)))
        x_high[a], x_low[a] = split(x)

    invert(1)
    invert(2)
    invert(0)

    lanes = lax.broadcasted_iota(jnp.int32, (NCON, 128), 1)
    down = lax.broadcasted_iota(jnp.int32, (NCON, 128), 0)
    identity = jnp.where(lax.rem(lanes, 64) == down, 1.0, 0.0)
    left_lanes = jnp.where(lanes < NCON, 1.0, 0.0)
    right_lanes = jnp.where((lanes >= 64) & (lanes < 64 + NCON), 1.0, 0.0)
    half_base = 64 * (lax.broadcasted_iota(jnp.int32, (8, 128), 1) // 64)
    blank = jnp.zeros((NCON, FACE), BF16)

    def column_of(slab, c):
        return jnp.take_along_axis(slab, half_base + (NCON + c), axis=1)

    def own_parts(a):
        return high[block(mine[a]), block(mine[a])], low[block(mine[a]), block(mine[a])]

    def other_parts(a):
        return other_high[a], other_low[a]

    def x_parts_of(a):
        return x_high[a], x_low[a]

    def refine(bases):
        systems, images = [], []
        for a in range(3):
            one, two = bases[a]
            both = jnp.concatenate(
                [product(split(one), other_parts(a)), product(split(two), own_parts(a))], axis=0
            )
            both = product(split(both), x_parts_of(a))
            one = split(product(split(both[:NCON]), own_parts(a)))
            two = split(product(split(both[NCON:]), other_parts(a)))
            gram = product(
                one, [jnp.concatenate([blank, part, blank, blank], axis=0) for part in one], NT
            )
            gram = gram + product(
                two, [jnp.concatenate([blank, blank, blank, part], axis=0) for part in two], NT
            )
            gram = gram + identity
            systems.append([gram[8 * v : 8 * v + 8] for v in range(4)])
            images.append([jnp.concatenate([p, blank, q, blank], axis=0) for p, q in zip(one, two)])
        eliminate(systems, column_of, 4, False)
        new = []
        for a in range(3):
            factor = jnp.concatenate(systems[a], axis=0)
            factor = jnp.concatenate([factor * left_lanes, factor * right_lanes], axis=0)
            both = product(split(factor), images[a])
            new.append((both[:NCON], both[NCON:]))
        return new

    for c in starts:
        c.wait_recv()
    bases = [(start[mine[a]], other_start[a]) for a in range(3)]
    for _ in range(SUB_ITERS):
        bases = refine(bases)
    returns = []
    for a in range(3):
        basis[mine[a]] = bases[a][0]
        basis[FACES + a] = bases[a][1]
        returns.append(copy(basis.at[FACES + a], basis.at[theirs[a]], behind[a]))

    def project(f, parts, columns):
        for g in columns:
            lower[block(f, NCON), block(g)] = product(
                parts, (high[block(f), block(g)], low[block(f), block(g)])
            )
        wide[block(f, NCON), block(f)] = basis[f]
        item[1, block(f, NCON), :] = product(parts, split(resid[block(f), :]))

    mix_copies = []
    for a in range(3):
        f = mine[a]
        parts = split(bases[a][0])
        side = product(parts, own_parts(a))
        lower[block(f, NCON), block(f)] = side
        facing = product(split(bases[a][1]), other_parts(a))
        both = product(split(jnp.concatenate([side, facing], axis=0)), x_parts_of(a))
        mixes[f] = both
        mixes[FACES + a] = jnp.concatenate([both[NCON:], both[:NCON]], axis=0)
        mix_copies.append(copy(mixes.at[FACES + a], mixes.at[theirs[a]], behind[a]))
        project(f, parts, mine[:a] + theirs)
    for a in range(3):
        returns[a].wait_recv()
        f = theirs[a]
        project(f, split(basis[f]), theirs[: a + 1])
    coarse = product(split(lower[...]), split(wide[...]), NT)
    blocks_row = lax.broadcasted_iota(jnp.int32, (COARSE, COARSE), 0) // NCON
    blocks_col = lax.broadcasted_iota(jnp.int32, (COARSE, COARSE), 1) // NCON
    coarse = coarse + jnp.where(blocks_row == blocks_col, 0.0, coarse).T
    item[0, 0:64, 0:64] = coarse[0:64, 0:64]
    item[0, 0:64, 64:128] = coarse[128:192, 128:192]
    item[0, 64:192, :] = coarse[64:192, 0:128]

    def six(ref, index):
        return ref.at[pl.ds(pl.multiple_of(index * 8, 8), 6), :]

    pl.semaphore_wait(plane_sem, GY - 1)
    for k in range(2):
        for c in range(32):
            pieces[8 * (32 * k + c) : 8 * (32 * k + c) + 6, :] = item[k, 6 * c : 6 * c + 6, :]
    scattered = [
        copy(six(pieces, 32 * to_core + to_chip), six(held, line), place)
        for to_core, to_chip, place in plane
    ]
    here_six = pl.ds(pl.multiple_of(line * 8, 8), 6)
    held[here_six, :] = pieces[pl.ds(pl.multiple_of((32 * core + chip) * 8, 8), 6), :]
    groups = jnp.broadcast_to(group_of[...].astype(F32), (64, 64))
    same = jnp.where(groups == groups.T, 1.0, 0.0).astype(BF16)
    for a in range(3):
        mix_copies[a].wait_recv()
    for f in range(FACES):
        mixed_high[f], mixed_low[f] = split(mixes[f].T)
    for c in scattered:
        c.wait_recv()
    for j in range(6):
        value = held[pl.ds(j, 64, stride=8), :]
        one = value.astype(BF16)
        rest = value - one.astype(F32)
        two = rest.astype(BF16)
        three = (rest - two.astype(F32)).astype(BF16)
        added = lax.dot_general(
            same, jnp.concatenate([one, two, three], axis=1), NN, preferred_element_type=F32
        )
        sums[pl.ds(j, 64, stride=8), :] = added[:, 0:128] + (added[:, 128:256] + added[:, 256:384])
    returned = [
        copy(six(sums, place[1] * GZ + place[2]), six(got, 32 * core + chip), place)
        for _, _, place in plane
    ]
    got[pl.ds(pl.multiple_of((32 * core + chip) * 8, 8), 6), :] = sums[here_six, :]
    for c in returned:
        c.wait_recv()
    for k in range(2):
        for c in range(32):
            total[k, 6 * c : 6 * c + 6, :] = got[8 * (32 * k + c) : 8 * (32 * k + c) + 6, :]

    system[:, 0:COLS] = total[1]
    packed = total[0]
    one = packed[0:64, 0:64]
    below = packed[64:192, 0:64]
    middle = packed[64:128, 64:128]
    final = packed[128:192, 64:128]
    corner = packed[0:64, 64:128]
    blank = jnp.zeros((64, 64), F32)
    system[0:64, COLS : COLS + 256] = jnp.concatenate([one, below.T, blank], axis=1)
    system[64:192, COLS : COLS + 256] = jnp.concatenate(
        [
            below,
            jnp.concatenate([middle, final], axis=0),
            jnp.concatenate([final.T, corner], axis=0),
            jnp.zeros((128, 64), F32),
        ],
        axis=1,
    )
    lanes = lax.broadcasted_iota(jnp.int32, (NCON, 128), 1)
    down = lax.broadcasted_iota(jnp.int32, (NCON, 128), 0)
    tall_lane = lax.broadcasted_iota(jnp.int32, (COARSE, 128), 1)
    tall_row = lax.broadcasted_iota(jnp.int32, (COARSE, 128), 0)

    def placed(block, offset):
        parts = []
        if offset:
            parts.append(jnp.zeros((offset, block.shape[1]), block.dtype))
        parts.append(block)
        if offset + NCON < 128:
            parts.append(jnp.zeros((128 - NCON - offset, block.shape[1]), block.dtype))
        return jnp.concatenate(parts, axis=0)

    for k in range(FACES):
        rows = slice(k * NCON, (k + 1) * NCON)
        tile = slice(COLS + 128 * (k // 4), COLS + 128 * (k // 4) + 128)
        place = (k % 4) * NCON
        unit = (place + NCON) % 128
        in_unit = (lanes >= unit) & (lanes < unit + NCON)
        in_place = (lanes >= place) & (lanes < place + NCON)
        block = jnp.where(in_place, system[rows, tile], 0.0)
        block = jnp.where(lanes == down + unit, 1.0, block)
        slabs = [block[8 * v : 8 * v + 8] for v in range(4)]
        eliminate(
            [slabs],
            lambda slab, c, place=place: jnp.broadcast_to(
                slab[:, place + c : place + c + 1], slab.shape
            ),
            16,
            True,
        )
        pivot_inverse = jnp.where(in_unit, jnp.concatenate(slabs, axis=0), 0.0)
        scaled = product(
            split(pivot_inverse), [placed(part, unit) for part in split(system[rows, :])]
        )
        column = split(
            jnp.where(
                (tall_lane >= place) & (tall_lane < place + NCON), system[:, tile], 0.0
            )
        )
        scaled_parts = [placed(part, place) for part in split(scaled)]
        system[rows, :] = scaled

        def clear(low_row, high_row):
            if low_row < high_row:
                update = product([part[low_row:high_row] for part in column], scaled_parts)
                system[low_row:high_row, :] = system[low_row:high_row, :] - update

        clear((k + 1) * NCON, min((k + 2) * NCON, COARSE))
        clear((k + 2) * NCON, COARSE)
        clear(0, k * NCON)
    answer[...] = system[:, 0:COLS].reshape(FACES, NCON, COLS)
    answers = [
        copy(answer.at[f], partner_answer.at[f ^ 1], across(f)) for f in range(FACES)
    ]
    for f in (2, 3, 4, 5, 0, 1):
        answers[f ^ 1].wait_recv()
        both = jnp.concatenate([answer[f], partner_answer[f]], axis=0)
        correction[f * FACE : (f + 1) * FACE, :] = product(
            (mixed_high[f], mixed_low[f]), split(both)
        )
    for a in range(3):
        for c in (faces[a], starts[a], returns[a], mix_copies[a]):
            c.wait_send()
    for c in scattered + returned + answers:
        c.wait_send()


def array(*shape):
    return jax.ShapeDtypeStruct(shape, F32)


def remote(collective_id):
    return pltpu.CompilerParams(collective_id=collective_id, has_side_effects=True)


DMA = pltpu.SemaphoreType.DMA


def per_device(schur, start_block, resid, group_of):
    matrix = schur[0, 0, 0]
    pairs = (3, FACE, FACE)
    copies = 12 + 2 * 63 + 6
    correction = pl.pallas_call(
        main_kernel,
        out_shape=array(ORDER, COLS),
        in_specs=[VMEM] + [ANY] * 3,
        out_specs=VMEM,
        scratch_shapes=[
            pltpu.VMEM(pairs, F32),
            pltpu.VMEM((3, FACE + 8, FACE // 2), F32),
            pltpu.VMEM((3, FACE + 8, FACE // 2), F32),
            pltpu.VMEM((ORDER, ORDER), F32),
            pltpu.VMEM((ORDER, ORDER), BF16),
            pltpu.VMEM((ORDER, ORDER), BF16),
            pltpu.VMEM(pairs, F32),
            pltpu.VMEM(pairs, BF16),
            pltpu.VMEM(pairs, BF16),
            pltpu.VMEM(pairs, BF16),
            pltpu.VMEM(pairs, BF16),
            pltpu.VMEM((FACES, NCON, FACE), F32),
            pltpu.VMEM((3, NCON, FACE), F32),
            pltpu.VMEM((ORDER, COLS), F32),
            pltpu.VMEM((FACES + 3, NCON, FACE), F32),
            pltpu.VMEM((COARSE, ORDER), F32),
            pltpu.VMEM((COARSE, ORDER), F32),
            pltpu.VMEM((2, COARSE, COLS), F32),
            pltpu.VMEM((FACES + 3, 2 * NCON, FACE), F32),
            pltpu.VMEM((FACES, FACE, 2 * NCON), BF16),
            pltpu.VMEM((FACES, FACE, 2 * NCON), BF16),
            pltpu.VMEM((512, COLS), F32),
            pltpu.VMEM((512, COLS), F32),
            pltpu.VMEM((512, COLS), F32),
            pltpu.VMEM((512, COLS), F32),
            pltpu.VMEM((2, COARSE, COLS), F32),
            pltpu.VMEM((COARSE, 384), F32),
            pltpu.VMEM((FACES, NCON, COLS), F32),
            pltpu.VMEM((FACES, NCON, COLS), F32),
            DMA((copies,)),
            DMA((copies,)),
            DMA((11,)),
            pltpu.SemaphoreType.REGULAR,
        ],
        compiler_params=remote(0),
        name="main",
    )(group_of[None], matrix, jnp.swapaxes(start_block[0, 0, 0], 1, 2), resid[0, 0, 0])
    return correction[None, None, None]


def solution(mesh):
    in_specs = (
        P("gx", "gy", "gz", None, None),
        P("gx", "gy", "gz", None, None, None),
        P("gx", "gy", "gz", None, None),
        P(),
    )
    out_specs = P("gx", "gy", "gz", None, None)
    return jax.shard_map(
        per_device, mesh=mesh, in_specs=in_specs, out_specs=out_specs, check_vma=False
    )
```

```python
import functools

import jax
import jax.numpy as jnp
from jax import lax
from jax.experimental import pallas as pl
from jax.experimental.pallas import tpu as pltpu
from jax.sharding import PartitionSpec as P

FACE = 256
NCON = 32
COLS = 128
FACES = 6
ORDER = FACE * FACES
COARSE = NCON * FACES
SUB_ITERS = 2
GX, GY, GZ = 4, 8, 8
MESH = pl.DeviceIdType.MESH
NN = (((1,), (0,)), ((), ()))
NT = (((1,), (1,)), ((), ()))
F32 = jnp.float32
BF16 = jnp.bfloat16
ANY = pl.BlockSpec(memory_space=pl.ANY)
VMEM = pl.BlockSpec(memory_space=pltpu.VMEM)
SMEM = pl.BlockSpec(memory_space=pltpu.SMEM)


def here():
    return lax.axis_index("gx"), lax.axis_index("gy"), lax.axis_index("gz")


def across(face):
    gx, gy, gz = here()
    step = 1 if face % 2 else -1
    if face < 2:
        return lax.rem(gx + step + GX, GX), gy, gz
    if face < 4:
        return gx, lax.rem(gy + step + GY, GY), gz
    return gx, gy, lax.rem(gz + step + GZ, GZ)


def send(src, dst, send_sem, recv_sem, device):
    return pltpu.make_async_remote_copy(
        src_ref=src,
        dst_ref=dst,
        send_sem=send_sem,
        recv_sem=recv_sem,
        device_id=device,
        device_id_type=MESH,
    )


def split(value):
    high = value.astype(BF16)
    return high, (value - high.astype(F32)).astype(BF16)


def product(left, right, dims=NN):
    (left_high, left_low), (right_high, right_low) = left, right
    rows = left_high.shape[0]
    both = lax.dot_general(
        jnp.concatenate([left_high, left_low], axis=0),
        right_high,
        dims,
        preferred_element_type=F32,
    )
    cross = lax.dot_general(left_high, right_low, dims, preferred_element_type=F32)
    return both[:rows] + (both[rows:] + cross)


def row_of(value, index):
    return jnp.broadcast_to(value[index : index + 1, :], value.shape)


def eliminate(systems, column_of, panel, inverse):
    sub = lax.broadcasted_iota(jnp.int32, (8, 128), 0)
    for first in range(0, NCON, panel):
        stop = first + panel
        low = 0 if inverse else first // 8
        spread = [
            {c: {v: column_of(slabs[v], c) for v in range(low, 4)} for c in range(first, stop)}
            for slabs in systems
        ]
        for j in range(first, stop):
            vj, sj = divmod(j, 8)
            for slabs, columns in zip(systems, spread):
                pivot = row_of(columns[j][vj], sj)
                invert = 1.0 / pivot
                row = row_of(slabs[vj], sj)
                scaled = row * invert
                rest = {c: row_of(columns[c][vj], sj) * invert for c in range(j + 1, stop)}
                done = scaled if inverse else row * lax.rsqrt(pivot)
                for v in range(0 if inverse else vj, 4):
                    factor = columns[j][v]
                    new = slabs[v] - factor * scaled
                    if v == vj:
                        new = jnp.where(sub == sj, done, new)
                        if not inverse and sj:
                            new = jnp.where(sub < sj, slabs[v], new)
                    slabs[v] = new
                    for c in range(j + 1, stop):
                        updated = columns[c][v] - factor * rest[c]
                        if inverse and v == vj:
                            updated = jnp.where(sub == sj, rest[c], updated)
                        columns[c][v] = updated


def main_kernel(
    group_of, schur_hbm, start_hbm, resid_hbm, correction,
    stage, packed_out, packed_in, schur, high, low, other, other_high, other_low, x_high, x_low, start, other_start, resid,
    basis, lower_high, lower_low, wide_high, wide_low, item, mixes, mixed_high, mixed_low,
    pieces, held, sums, got, total, system, answer, partner_answer,
    send_sem, recv_sem, load_sem, plane_sem,
):
    gx, gy, gz = here()
    core = lax.rem(gy, 2)
    turns = (core, 0, core)
    mine = [2 * a + turns[a] for a in range(3)]
    theirs = [2 * a + 1 - turns[a] for a in range(3)]

    def along(a, step):
        if a == 0:
            return lax.rem(gx + step + GX, GX), gy, gz
        if a == 1:
            return gx, lax.rem(gy + step + GY, GY), gz
        return gx, gy, lax.rem(gz + step + GZ, GZ)

    ahead = [along(a, 1 - 2 * turns[a]) for a in range(3)]
    behind = [along(a, 2 * turns[a] - 1) for a in range(3)]
    x = gy // 2
    y, z = gz // 2, lax.rem(gz, 2)

    def plane_device(i, cc):
        to_x, to_y, to_z = lax.rem(x + i % 4, 4), lax.rem(y + (i // 4) % 4, 4), lax.rem(z + i // 16, 2)
        to_core = core + cc * (1 - 2 * core)
        return to_core, (to_x * 4 + to_y) * 2 + to_z, (gx, 2 * to_x + to_core, 2 * to_y + to_z)

    chip = (x * 4 + y) * 2 + z
    line = gy * GZ + gz
    hops = {i: (i % 4) * (4 - i % 4) + (i // 4 % 4) * (4 - i // 4 % 4) + 3 * (i // 16) for i in range(32)}
    far_first = sorted(range(32), key=lambda i: -hops[i])
    plane = [plane_device(i, cc) for i in far_first for cc in range(2) if i or cc]

    def block(f, size=FACE):
        return pl.ds(pl.multiple_of(f * size, size), size)

    loads = []

    def load(src, dst):
        copy = pltpu.make_async_copy(src, dst, load_sem.at[len(loads)])
        copy.start()
        loads.append(copy)

    for a in range(3):
        load(schur_hbm.at[block(theirs[a]), block(theirs[a])], stage.at[a])
    barrier = pltpu.get_barrier_semaphore()
    row_devices = [(gx, lax.rem(gy + i, GY), gz) for i in range(1, GY)]
    column_devices = [(gx, gy, lax.rem(gz + i, GZ)) for i in range(1, GZ)]
    greeted = [ahead[0], behind[0]] + row_devices + column_devices
    for device in greeted:
        pl.semaphore_signal(barrier, inc=1, device_id=device, device_id_type=MESH)
    for f in range(FACES):
        rows = pl.ds(f * FACE, FACE)
        load(schur_hbm.at[rows, :], schur.at[rows, :])
    load(start_hbm, start)
    load(resid_hbm, resid)
    half = FACE // 2
    half_rows = lax.broadcasted_iota(jnp.int32, (half, half), 0)
    half_cols = lax.broadcasted_iota(jnp.int32, (half, half), 1)
    for a in range(3):
        loads[a].wait()
        first_block = stage[a, 0:half, 0:half]
        second_block = stage[a, half:FACE, half:FACE]
        packed_out[a, 0:half] = stage[a, half:FACE, 0:half]
        packed_out[a, half:FACE] = jnp.where(half_rows >= half_cols, first_block, second_block)
        packed_out[a, FACE : FACE + 8] = jnp.broadcast_to(
            jnp.sum(
                jnp.where(half_rows == half_cols, second_block, 0.0), axis=0, keepdims=True
            ),
            (8, half),
        )
    pl.semaphore_wait(barrier, len(greeted))
    for device in row_devices:
        pl.semaphore_signal(plane_sem, inc=1, device_id=device, device_id_type=MESH)
    counter = [0]

    def copy(src, dst, device):
        n = counter[0]
        counter[0] += 1
        started = send(src, dst, send_sem.at[n], recv_sem.at[n], device)
        started.start()
        return started

    faces = {a: copy(packed_out.at[a], packed_in.at[a], ahead[a]) for a in (2, 0, 1)}
    starts = [copy(start_hbm.at[theirs[a]], other_start.at[a], ahead[a]) for a in range(3)]

    def divide(r, carry):
        rows = pl.ds(pl.multiple_of(r * 64, 64), 64)
        high[rows, :], low[rows, :] = split(schur[rows, :])
        return carry

    for ref in (lower_high, lower_low, wide_high, wide_low):
        ref[...] = jnp.zeros_like(ref)
    for f in range(FACES):
        loads[3 + f].wait()
        lax.fori_loop(f * 4, f * 4 + 4, divide, 0)
    loads[9].wait()
    loads[10].wait()

    row_ids = lax.broadcasted_iota(jnp.int32, (FACE, FACE), 0)
    col_ids = lax.broadcasted_iota(jnp.int32, (FACE, FACE), 1)

    def invert(a):
        faces[a].wait_recv()
        below = packed_in[a, 0:half]
        folded = packed_in[a, half:FACE]
        mirrored = folded.T
        second_diagonal = jnp.broadcast_to(packed_in[a, FACE : FACE + 1], (half, half))
        other[a, half:FACE, 0:half] = below
        other[a, 0:half, half:FACE] = below.T
        other[a, 0:half, 0:half] = jnp.where(half_rows >= half_cols, folded, mirrored)
        other[a, half:FACE, half:FACE] = jnp.where(
            half_rows < half_cols,
            folded,
            jnp.where(half_rows == half_cols, second_diagonal, mirrored),
        )
        theirs_block = other[a]
        other_high[a], other_low[a] = split(theirs_block)
        total = schur[block(mine[a]), block(mine[a])] + theirs_block
        diagonal = jnp.where(row_ids == col_ids, total, 0.0)
        across_row = 1.0 / jnp.sum(diagonal, axis=0, keepdims=True)
        down_col = 1.0 / jnp.sum(diagonal, axis=1, keepdims=True)
        total_parts = split(total)
        x = jnp.where(row_ids == col_ids, 2.0 * across_row, 0.0) - total * across_row * down_col
        for _ in range(2):
            x_parts = split(x)
            x = 2.0 * x - product(x_parts, split(product(total_parts, x_parts)))
        x_high[a], x_low[a] = split(x)

    invert(1)
    invert(2)
    invert(0)

    lanes = lax.broadcasted_iota(jnp.int32, (NCON, 128), 1)
    down = lax.broadcasted_iota(jnp.int32, (NCON, 128), 0)
    identity = jnp.where(lax.rem(lanes, 64) == down, 1.0, 0.0)
    left_lanes = jnp.where(lanes < NCON, 1.0, 0.0)
    right_lanes = jnp.where((lanes >= 64) & (lanes < 64 + NCON), 1.0, 0.0)
    half_base = 64 * (lax.broadcasted_iota(jnp.int32, (8, 128), 1) // 64)
    blank = jnp.zeros((NCON, FACE), BF16)

    def column_of(slab, c):
        return jnp.take_along_axis(slab, half_base + (NCON + c), axis=1)

    def own_parts(a):
        return high[block(mine[a]), block(mine[a])], low[block(mine[a]), block(mine[a])]

    def other_parts(a):
        return other_high[a], other_low[a]

    def x_parts_of(a):
        return x_high[a], x_low[a]

    def refine(bases):
        systems, images = [], []
        values = [
            jnp.concatenate(
                [
                    product(split(bases[a][0]), other_parts(a)),
                    product(split(bases[a][1]), own_parts(a)),
                ],
                axis=0,
            )
            for a in range(3)
        ]
        values = [product(split(values[a]), x_parts_of(a)) for a in range(3)]
        values = [
            (
                split(product(split(values[a][:NCON]), own_parts(a))),
                split(product(split(values[a][NCON:]), other_parts(a))),
            )
            for a in range(3)
        ]
        for one, two in values:
            gram = product(
                one, [jnp.concatenate([blank, part, blank, blank], axis=0) for part in one], NT
            )
            gram = gram + product(
                two, [jnp.concatenate([blank, blank, blank, part], axis=0) for part in two], NT
            )
            gram = gram + identity
            systems.append([gram[8 * v : 8 * v + 8] for v in range(4)])
            images.append([jnp.concatenate([p, blank, q, blank], axis=0) for p, q in zip(one, two)])
        eliminate(systems, column_of, 4, False)
        new = []
        for a in range(3):
            factor = jnp.concatenate(systems[a], axis=0)
            factor = jnp.concatenate([factor * left_lanes, factor * right_lanes], axis=0)
            both = product(split(factor), images[a])
            new.append((both[:NCON], both[NCON:]))
        return new

    for c in starts:
        c.wait_recv()
    bases = [(start[mine[a]], other_start[a]) for a in range(3)]
    for _ in range(SUB_ITERS):
        bases = refine(bases)
    returns = []
    for a in range(3):
        basis[mine[a]] = bases[a][0]
        basis[FACES + a] = bases[a][1]
        returns.append(copy(basis.at[FACES + a], basis.at[theirs[a]], behind[a]))

    def project(f, parts, columns):
        rows = block(f, NCON)
        for g in columns:
            lower_high[rows, block(g)], lower_low[rows, block(g)] = split(
                product(parts, (high[block(f), block(g)], low[block(f), block(g)]))
            )
        wide_high[rows, block(f)], wide_low[rows, block(f)] = parts
        item[1, rows, :] = product(parts, split(resid[block(f), :]))

    mix_copies = []
    for a in range(3):
        f = mine[a]
        parts = split(bases[a][0])
        side = product(parts, own_parts(a))
        lower_high[block(f, NCON), block(f)], lower_low[block(f, NCON), block(f)] = split(side)
        facing = product(split(bases[a][1]), other_parts(a))
        both = product(split(jnp.concatenate([side, facing], axis=0)), x_parts_of(a))
        mixes[f] = both
        mixes[FACES + a] = jnp.concatenate([both[NCON:], both[:NCON]], axis=0)
        mix_copies.append(copy(mixes.at[FACES + a], mixes.at[theirs[a]], behind[a]))
        project(f, parts, mine[:a] + theirs)
    for a in range(3):
        returns[a].wait_recv()
        f = theirs[a]
        project(f, split(basis[f]), theirs[: a + 1])
    coarse = product(
        (lower_high[...], lower_low[...]), (wide_high[...], wide_low[...]), NT
    )
    blocks_row = lax.broadcasted_iota(jnp.int32, (COARSE, COARSE), 0) // NCON
    blocks_col = lax.broadcasted_iota(jnp.int32, (COARSE, COARSE), 1) // NCON
    coarse = coarse + jnp.where(blocks_row == blocks_col, 0.0, coarse).T
    item[0, 0:64, 0:64] = coarse[0:64, 0:64]
    item[0, 0:64, 64:128] = coarse[128:192, 128:192]
    item[0, 64:192, :] = coarse[64:192, 0:128]

    def six(ref, index):
        return ref.at[pl.ds(pl.multiple_of(index * 8, 8), 6), :]

    pl.semaphore_wait(plane_sem, GY - 1)
    for k in range(2):
        for c in range(32):
            pieces[8 * (32 * k + c) : 8 * (32 * k + c) + 6, :] = item[k, 6 * c : 6 * c + 6, :]
    scattered = [
        copy(six(pieces, 32 * to_core + to_chip), six(held, line), place)
        for to_core, to_chip, place in plane
    ]
    here_six = pl.ds(pl.multiple_of(line * 8, 8), 6)
    held[here_six, :] = pieces[pl.ds(pl.multiple_of((32 * core + chip) * 8, 8), 6), :]
    groups = jnp.broadcast_to(group_of[...].astype(F32), (64, 64))
    same = jnp.where(groups == groups.T, 1.0, 0.0).astype(BF16)
    for a in range(3):
        mix_copies[a].wait_recv()
    for f in range(FACES):
        mixed_high[f], mixed_low[f] = split(mixes[f].T)
    for c in scattered:
        c.wait_recv()
    for j in range(6):
        value = held[pl.ds(j, 64, stride=8), :]
        one = value.astype(BF16)
        rest = value - one.astype(F32)
        two = rest.astype(BF16)
        three = (rest - two.astype(F32)).astype(BF16)
        added = lax.dot_general(
            same, jnp.concatenate([one, two, three], axis=1), NN, preferred_element_type=F32
        )
        sums[pl.ds(j, 64, stride=8), :] = added[:, 0:128] + (added[:, 128:256] + added[:, 256:384])
    returned = [
        copy(six(sums, place[1] * GZ + place[2]), six(got, 32 * core + chip), place)
        for _, _, place in plane
    ]
    got[pl.ds(pl.multiple_of((32 * core + chip) * 8, 8), 6), :] = sums[here_six, :]
    for c in returned:
        c.wait_recv()
    for k in range(2):
        for c in range(32):
            total[k, 6 * c : 6 * c + 6, :] = got[8 * (32 * k + c) : 8 * (32 * k + c) + 6, :]

    system[:, 0:COLS] = total[1]
    packed = total[0]
    one = packed[0:64, 0:64]
    below = packed[64:192, 0:64]
    middle = packed[64:128, 64:128]
    final = packed[128:192, 64:128]
    corner = packed[0:64, 64:128]
    blank = jnp.zeros((64, 64), F32)
    system[0:64, COLS : COLS + 256] = jnp.concatenate([one, below.T, blank], axis=1)
    system[64:192, COLS : COLS + 256] = jnp.concatenate(
        [
            below,
            jnp.concatenate([middle, final], axis=0),
            jnp.concatenate([final.T, corner], axis=0),
            jnp.zeros((128, 64), F32),
        ],
        axis=1,
    )
    lanes = lax.broadcasted_iota(jnp.int32, (NCON, 128), 1)
    down = lax.broadcasted_iota(jnp.int32, (NCON, 128), 0)
    tall_lane = lax.broadcasted_iota(jnp.int32, (COARSE, 128), 1)
    tall_row = lax.broadcasted_iota(jnp.int32, (COARSE, 128), 0)

    def placed(block, offset):
        parts = []
        if offset:
            parts.append(jnp.zeros((offset, block.shape[1]), block.dtype))
        parts.append(block)
        if offset + NCON < 128:
            parts.append(jnp.zeros((128 - NCON - offset, block.shape[1]), block.dtype))
        return jnp.concatenate(parts, axis=0)

    for k in range(FACES):
        rows = slice(k * NCON, (k + 1) * NCON)
        live = slice(0, COLS if k == FACES - 1 else 384)
        tile = slice(COLS + 128 * (k // 4), COLS + 128 * (k // 4) + 128)
        place = (k % 4) * NCON
        unit = (place + NCON) % 128
        in_unit = (lanes >= unit) & (lanes < unit + NCON)
        in_place = (lanes >= place) & (lanes < place + NCON)
        block = jnp.where(in_place, system[rows, tile], 0.0)
        block = jnp.where(lanes == down + unit, 1.0, block)
        slabs = [block[8 * v : 8 * v + 8] for v in range(4)]
        eliminate(
            [slabs],
            lambda slab, c, place=place: jnp.broadcast_to(
                slab[:, place + c : place + c + 1], slab.shape
            ),
            16,
            True,
        )
        pivot_inverse = jnp.where(in_unit, jnp.concatenate(slabs, axis=0), 0.0)
        scaled = product(
            split(pivot_inverse), [placed(part, unit) for part in split(system[rows, live])]
        )
        column = split(
            jnp.where(
                (tall_lane >= place) & (tall_lane < place + NCON), system[:, tile], 0.0
            )
        )
        scaled_parts = [placed(part, place) for part in split(scaled)]
        system[rows, live] = scaled

        def clear(low_row, high_row):
            if low_row < high_row:
                update = product([part[low_row:high_row] for part in column], scaled_parts)
                system[low_row:high_row, live] = system[low_row:high_row, live] - update

        clear((k + 1) * NCON, min((k + 2) * NCON, COARSE))
        clear((k + 2) * NCON, COARSE)
        clear(0, k * NCON)
    answer[...] = system[:, 0:COLS].reshape(FACES, NCON, COLS)
    answers = [
        copy(answer.at[f], partner_answer.at[f ^ 1], across(f)) for f in range(FACES)
    ]
    for f in (2, 3, 4, 5, 0, 1):
        answers[f ^ 1].wait_recv()
        both = jnp.concatenate([answer[f], partner_answer[f]], axis=0)
        correction[f * FACE : (f + 1) * FACE, :] = product(
            (mixed_high[f], mixed_low[f]), split(both)
        )
    for a in range(3):
        for c in (faces[a], starts[a], returns[a], mix_copies[a]):
            c.wait_send()
    for c in scattered + returned + answers:
        c.wait_send()


def array(*shape):
    return jax.ShapeDtypeStruct(shape, F32)


def remote(collective_id):
    return pltpu.CompilerParams(collective_id=collective_id, has_side_effects=True)


DMA = pltpu.SemaphoreType.DMA


def per_device(schur, start_block, resid, group_of):
    matrix = schur[0, 0, 0]
    pairs = (3, FACE, FACE)
    copies = 12 + 2 * 63 + 6
    correction = pl.pallas_call(
        main_kernel,
        out_shape=array(ORDER, COLS),
        in_specs=[VMEM] + [ANY] * 3,
        out_specs=VMEM,
        scratch_shapes=[
            pltpu.VMEM(pairs, F32),
            pltpu.VMEM((3, FACE + 8, FACE // 2), F32),
            pltpu.VMEM((3, FACE + 8, FACE // 2), F32),
            pltpu.VMEM((ORDER, ORDER), F32),
            pltpu.VMEM((ORDER, ORDER), BF16),
            pltpu.VMEM((ORDER, ORDER), BF16),
            pltpu.VMEM(pairs, F32),
            pltpu.VMEM(pairs, BF16),
            pltpu.VMEM(pairs, BF16),
            pltpu.VMEM(pairs, BF16),
            pltpu.VMEM(pairs, BF16),
            pltpu.VMEM((FACES, NCON, FACE), F32),
            pltpu.VMEM((3, NCON, FACE), F32),
            pltpu.VMEM((ORDER, COLS), F32),
            pltpu.VMEM((FACES + 3, NCON, FACE), F32),
            pltpu.VMEM((COARSE, ORDER), BF16),
            pltpu.VMEM((COARSE, ORDER), BF16),
            pltpu.VMEM((COARSE, ORDER), BF16),
            pltpu.VMEM((COARSE, ORDER), BF16),
            pltpu.VMEM((2, COARSE, COLS), F32),
            pltpu.VMEM((FACES + 3, 2 * NCON, FACE), F32),
            pltpu.VMEM((FACES, FACE, 2 * NCON), BF16),
            pltpu.VMEM((FACES, FACE, 2 * NCON), BF16),
            pltpu.VMEM((512, COLS), F32),
            pltpu.VMEM((512, COLS), F32),
            pltpu.VMEM((512, COLS), F32),
            pltpu.VMEM((512, COLS), F32),
            pltpu.VMEM((2, COARSE, COLS), F32),
            pltpu.VMEM((COARSE, 384), F32),
            pltpu.VMEM((FACES, NCON, COLS), F32),
            pltpu.VMEM((FACES, NCON, COLS), F32),
            DMA((copies,)),
            DMA((copies,)),
            DMA((11,)),
            pltpu.SemaphoreType.REGULAR,
        ],
        compiler_params=remote(0),
        name="main",
    )(group_of[None], matrix, jnp.swapaxes(start_block[0, 0, 0], 1, 2), resid[0, 0, 0])
    return correction[None, None, None]


def solution(mesh):
    in_specs = (
        P("gx", "gy", "gz", None, None),
        P("gx", "gy", "gz", None, None, None),
        P("gx", "gy", "gz", None, None),
        P(),
    )
    out_specs = P("gx", "gy", "gz", None, None)
    return jax.shard_map(
        per_device, mesh=mesh, in_specs=in_specs, out_specs=out_specs, check_vma=False
    )
```

```python
import functools

import jax
import jax.numpy as jnp
from jax import lax
from jax.experimental import pallas as pl
from jax.experimental.pallas import tpu as pltpu
from jax.sharding import PartitionSpec as P

FACE = 256
NCON = 32
COLS = 128
FACES = 6
ORDER = FACE * FACES
COARSE = NCON * FACES
SUB_ITERS = 2
GX, GY, GZ = 4, 8, 8
MESH = pl.DeviceIdType.MESH
NN = (((1,), (0,)), ((), ()))
NT = (((1,), (1,)), ((), ()))
F32 = jnp.float32
BF16 = jnp.bfloat16
ANY = pl.BlockSpec(memory_space=pl.ANY)
VMEM = pl.BlockSpec(memory_space=pltpu.VMEM)
SMEM = pl.BlockSpec(memory_space=pltpu.SMEM)


def here():
    return lax.axis_index("gx"), lax.axis_index("gy"), lax.axis_index("gz")


def across(face):
    gx, gy, gz = here()
    step = 1 if face % 2 else -1
    if face < 2:
        return lax.rem(gx + step + GX, GX), gy, gz
    if face < 4:
        return gx, lax.rem(gy + step + GY, GY), gz
    return gx, gy, lax.rem(gz + step + GZ, GZ)


def send(src, dst, send_sem, recv_sem, device):
    return pltpu.make_async_remote_copy(
        src_ref=src,
        dst_ref=dst,
        send_sem=send_sem,
        recv_sem=recv_sem,
        device_id=device,
        device_id_type=MESH,
    )


def split(value):
    high = value.astype(BF16)
    return high, (value - high.astype(F32)).astype(BF16)


def product(left, right, dims=NN):
    (left_high, left_low), (right_high, right_low) = left, right
    rows = left_high.shape[0]
    both = lax.dot_general(
        jnp.concatenate([left_high, left_low], axis=0),
        right_high,
        dims,
        preferred_element_type=F32,
    )
    cross = lax.dot_general(left_high, right_low, dims, preferred_element_type=F32)
    return both[:rows] + (both[rows:] + cross)


def row_of(value, index):
    return jnp.broadcast_to(value[index : index + 1, :], value.shape)


def eliminate(systems, column_of, panel, inverse):
    sub = lax.broadcasted_iota(jnp.int32, (8, 128), 0)
    for first in range(0, NCON, panel):
        stop = first + panel
        low = 0 if inverse else first // 8
        spread = [
            {c: {v: column_of(slabs[v], c) for v in range(low, 4)} for c in range(first, stop)}
            for slabs in systems
        ]
        for j in range(first, stop):
            vj, sj = divmod(j, 8)
            for slabs, columns in zip(systems, spread):
                pivot = row_of(columns[j][vj], sj)
                invert = 1.0 / pivot
                row = row_of(slabs[vj], sj)
                scaled = row * invert
                rest = {c: row_of(columns[c][vj], sj) * invert for c in range(j + 1, stop)}
                done = scaled if inverse else row * lax.rsqrt(pivot)
                for v in range(0 if inverse else vj, 4):
                    factor = columns[j][v]
                    new = slabs[v] - factor * scaled
                    if v == vj:
                        new = jnp.where(sub == sj, done, new)
                        if not inverse and sj:
                            new = jnp.where(sub < sj, slabs[v], new)
                    slabs[v] = new
                    for c in range(j + 1, stop):
                        updated = columns[c][v] - factor * rest[c]
                        if inverse and v == vj:
                            updated = jnp.where(sub == sj, rest[c], updated)
                        columns[c][v] = updated


def main_kernel(
    group_of, schur_hbm, start_hbm, resid_hbm, correction,
    stage, packed_out, packed_in, schur, high, low, other, other_high, other_low, x_high, x_low, start, other_start, resid,
    basis, lower_high, lower_low, wide_high, wide_low, item, mixes, mixed_high, mixed_low,
    pieces, held, sums, got, total, system, answer, partner_answer,
    send_sem, recv_sem, load_sem, plane_sem,
):
    gx, gy, gz = here()
    core = lax.rem(gy, 2)
    turns = (core, 0, core)
    mine = [2 * a + turns[a] for a in range(3)]
    theirs = [2 * a + 1 - turns[a] for a in range(3)]

    def along(a, step):
        if a == 0:
            return lax.rem(gx + step + GX, GX), gy, gz
        if a == 1:
            return gx, lax.rem(gy + step + GY, GY), gz
        return gx, gy, lax.rem(gz + step + GZ, GZ)

    ahead = [along(a, 1 - 2 * turns[a]) for a in range(3)]
    behind = [along(a, 2 * turns[a] - 1) for a in range(3)]
    x = gy // 2
    y, z = gz // 2, lax.rem(gz, 2)

    def plane_device(i, cc):
        to_x, to_y, to_z = lax.rem(x + i % 4, 4), lax.rem(y + (i // 4) % 4, 4), lax.rem(z + i // 16, 2)
        to_core = core + cc * (1 - 2 * core)
        return to_core, (to_x * 4 + to_y) * 2 + to_z, (gx, 2 * to_x + to_core, 2 * to_y + to_z)

    chip = (x * 4 + y) * 2 + z
    line = gy * GZ + gz
    hops = {i: (i % 4) * (4 - i % 4) + (i // 4 % 4) * (4 - i // 4 % 4) + 3 * (i // 16) for i in range(32)}
    far_first = sorted(range(32), key=lambda i: -hops[i])
    plane = [plane_device(i, cc) for i in far_first for cc in range(2) if i or cc]

    def block(f, size=FACE):
        return pl.ds(pl.multiple_of(f * size, size), size)

    loads = []

    def load(src, dst):
        copy = pltpu.make_async_copy(src, dst, load_sem.at[len(loads)])
        copy.start()
        loads.append(copy)

    for a in range(3):
        load(schur_hbm.at[block(theirs[a]), block(theirs[a])], stage.at[a])
    barrier = pltpu.get_barrier_semaphore()
    row_devices = [(gx, lax.rem(gy + i, GY), gz) for i in range(1, GY)]
    column_devices = [(gx, gy, lax.rem(gz + i, GZ)) for i in range(1, GZ)]
    greeted = [ahead[0], behind[0]] + row_devices + column_devices
    for device in greeted:
        pl.semaphore_signal(barrier, inc=1, device_id=device, device_id_type=MESH)
    for f in range(FACES):
        rows = pl.ds(f * FACE, FACE)
        load(schur_hbm.at[rows, :], schur.at[rows, :])
    load(start_hbm, start)
    load(resid_hbm, resid)
    half = FACE // 2
    half_rows = lax.broadcasted_iota(jnp.int32, (half, half), 0)
    half_cols = lax.broadcasted_iota(jnp.int32, (half, half), 1)
    for a in range(3):
        loads[a].wait()
        first_block = stage[a, 0:half, 0:half]
        second_block = stage[a, half:FACE, half:FACE]
        packed_out[a, 0:half] = stage[a, half:FACE, 0:half]
        packed_out[a, half:FACE] = jnp.where(half_rows >= half_cols, first_block, second_block)
        packed_out[a, FACE : FACE + 8] = jnp.broadcast_to(
            jnp.sum(
                jnp.where(half_rows == half_cols, second_block, 0.0), axis=0, keepdims=True
            ),
            (8, half),
        )
    pl.semaphore_wait(barrier, len(greeted))
    for device in row_devices:
        pl.semaphore_signal(plane_sem, inc=1, device_id=device, device_id_type=MESH)
    counter = [0]

    def copy(src, dst, device):
        n = counter[0]
        counter[0] += 1
        started = send(src, dst, send_sem.at[n], recv_sem.at[n], device)
        started.start()
        return started

    faces = {a: copy(packed_out.at[a], packed_in.at[a], ahead[a]) for a in (2, 0, 1)}
    starts = [copy(start_hbm.at[theirs[a]], other_start.at[a], ahead[a]) for a in range(3)]

    def divide(r, carry):
        rows = pl.ds(pl.multiple_of(r * 64, 64), 64)
        high[rows, :], low[rows, :] = split(schur[rows, :])
        return carry

    for ref in (lower_high, lower_low, wide_high, wide_low):
        ref[...] = jnp.zeros_like(ref)
    for f in range(FACES):
        loads[3 + f].wait()
        lax.fori_loop(f * 4, f * 4 + 4, divide, 0)
    loads[9].wait()
    loads[10].wait()

    row_ids = lax.broadcasted_iota(jnp.int32, (FACE, FACE), 0)
    col_ids = lax.broadcasted_iota(jnp.int32, (FACE, FACE), 1)

    def invert(a):
        faces[a].wait_recv()
        below = packed_in[a, 0:half]
        folded = packed_in[a, half:FACE]
        mirrored = folded.T
        second_diagonal = jnp.broadcast_to(packed_in[a, FACE : FACE + 1], (half, half))
        other[a, half:FACE, 0:half] = below
        other[a, 0:half, half:FACE] = below.T
        other[a, 0:half, 0:half] = jnp.where(half_rows >= half_cols, folded, mirrored)
        other[a, half:FACE, half:FACE] = jnp.where(
            half_rows < half_cols,
            folded,
            jnp.where(half_rows == half_cols, second_diagonal, mirrored),
        )
        theirs_block = other[a]
        other_high[a], other_low[a] = split(theirs_block)
        total = schur[block(mine[a]), block(mine[a])] + theirs_block
        diagonal = jnp.where(row_ids == col_ids, total, 0.0)
        across_row = 1.0 / jnp.sum(diagonal, axis=0, keepdims=True)
        down_col = 1.0 / jnp.sum(diagonal, axis=1, keepdims=True)
        total_parts = split(total)
        x = jnp.where(row_ids == col_ids, 2.0 * across_row, 0.0) - total * across_row * down_col
        for _ in range(2):
            x_parts = split(x)
            x = 2.0 * x - product(x_parts, split(product(total_parts, x_parts)))
        x_high[a], x_low[a] = split(x)

    invert(1)
    invert(2)
    invert(0)

    lanes = lax.broadcasted_iota(jnp.int32, (NCON, 128), 1)
    down = lax.broadcasted_iota(jnp.int32, (NCON, 128), 0)
    identity = jnp.where(lax.rem(lanes, 64) == down, 1.0, 0.0)
    left_lanes = jnp.where(lanes < NCON, 1.0, 0.0)
    right_lanes = jnp.where((lanes >= 64) & (lanes < 64 + NCON), 1.0, 0.0)
    half_base = 64 * (lax.broadcasted_iota(jnp.int32, (8, 128), 1) // 64)
    blank = jnp.zeros((NCON, FACE), BF16)

    def column_of(slab, c):
        return jnp.take_along_axis(slab, half_base + (NCON + c), axis=1)

    def own_parts(a):
        return high[block(mine[a]), block(mine[a])], low[block(mine[a]), block(mine[a])]

    def other_parts(a):
        return other_high[a], other_low[a]

    def x_parts_of(a):
        return x_high[a], x_low[a]

    def refine(bases):
        systems, images = [], []
        values = [
            jnp.concatenate(
                [
                    product(split(bases[a][0]), other_parts(a)),
                    product(split(bases[a][1]), own_parts(a)),
                ],
                axis=0,
            )
            for a in range(3)
        ]
        values = [product(split(values[a]), x_parts_of(a)) for a in range(3)]
        values = [
            (
                split(product(split(values[a][:NCON]), own_parts(a))),
                split(product(split(values[a][NCON:]), other_parts(a))),
            )
            for a in range(3)
        ]
        for one, two in values:
            gram = product(
                one, [jnp.concatenate([blank, part, blank, blank], axis=0) for part in one], NT
            )
            gram = gram + product(
                two, [jnp.concatenate([blank, blank, blank, part], axis=0) for part in two], NT
            )
            gram = gram + identity
            systems.append([gram[8 * v : 8 * v + 8] for v in range(4)])
            images.append([jnp.concatenate([p, blank, q, blank], axis=0) for p, q in zip(one, two)])
        eliminate(systems, column_of, 4, False)
        new = []
        for a in range(3):
            factor = jnp.concatenate(systems[a], axis=0)
            factor = jnp.concatenate([factor * left_lanes, factor * right_lanes], axis=0)
            both = product(split(factor), images[a])
            new.append((both[:NCON], both[NCON:]))
        return new

    for c in starts:
        c.wait_recv()
    bases = [(start[mine[a]], other_start[a]) for a in range(3)]
    for _ in range(SUB_ITERS):
        bases = refine(bases)
    returns = []
    for a in range(3):
        basis[mine[a]] = bases[a][0]
        basis[FACES + a] = bases[a][1]
        returns.append(copy(basis.at[FACES + a], basis.at[theirs[a]], behind[a]))

    def project(f, parts, columns):
        rows = block(f, NCON)
        for g in columns:
            lower_high[rows, block(g)], lower_low[rows, block(g)] = split(
                product(parts, (high[block(f), block(g)], low[block(f), block(g)]))
            )
        wide_high[rows, block(f)], wide_low[rows, block(f)] = parts
        item[1, rows, :] = product(parts, split(resid[block(f), :]))

    mix_copies = []
    parts = [split(bases[a][0]) for a in range(3)]
    sides = [product(parts[a], own_parts(a)) for a in range(3)]
    facing = [product(split(bases[a][1]), other_parts(a)) for a in range(3)]
    both = [
        product(split(jnp.concatenate([sides[a], facing[a]], axis=0)), x_parts_of(a))
        for a in range(3)
    ]
    for a in range(3):
        f = mine[a]
        rows = block(f, NCON)
        lower_high[rows, block(f)], lower_low[rows, block(f)] = split(sides[a])
        mixes[f] = both[a]
        mixes[FACES + a] = jnp.concatenate([both[a][NCON:], both[a][:NCON]], axis=0)
        mix_copies.append(copy(mixes.at[FACES + a], mixes.at[theirs[a]], behind[a]))
    for a in range(3):
        project(mine[a], parts[a], mine[:a] + theirs)
    for a in range(3):
        returns[a].wait_recv()
        f = theirs[a]
        project(f, split(basis[f]), theirs[: a + 1])
    coarse = product(
        (lower_high[...], lower_low[...]), (wide_high[...], wide_low[...]), NT
    )
    blocks_row = lax.broadcasted_iota(jnp.int32, (COARSE, COARSE), 0) // NCON
    blocks_col = lax.broadcasted_iota(jnp.int32, (COARSE, COARSE), 1) // NCON
    coarse = coarse + jnp.where(blocks_row == blocks_col, 0.0, coarse).T
    item[0, 0:64, 0:64] = coarse[0:64, 0:64]
    item[0, 0:64, 64:128] = coarse[128:192, 128:192]
    item[0, 64:192, :] = coarse[64:192, 0:128]

    def six(ref, index):
        return ref.at[pl.ds(pl.multiple_of(index * 8, 8), 6), :]

    pl.semaphore_wait(plane_sem, GY - 1)
    for k in range(2):
        for c in range(32):
            pieces[8 * (32 * k + c) : 8 * (32 * k + c) + 6, :] = item[k, 6 * c : 6 * c + 6, :]
    scattered = [
        copy(six(pieces, 32 * to_core + to_chip), six(held, line), place)
        for to_core, to_chip, place in plane
    ]
    here_six = pl.ds(pl.multiple_of(line * 8, 8), 6)
    held[here_six, :] = pieces[pl.ds(pl.multiple_of((32 * core + chip) * 8, 8), 6), :]
    groups = jnp.broadcast_to(group_of[...].astype(F32), (64, 64))
    same = jnp.where(groups == groups.T, 1.0, 0.0).astype(BF16)
    for a in range(3):
        mix_copies[a].wait_recv()
    for f in range(FACES):
        mixed_high[f], mixed_low[f] = split(mixes[f].T)
    for c in scattered:
        c.wait_recv()
    for j in range(6):
        value = held[pl.ds(j, 64, stride=8), :]
        one = value.astype(BF16)
        rest = value - one.astype(F32)
        two = rest.astype(BF16)
        three = (rest - two.astype(F32)).astype(BF16)
        added = lax.dot_general(
            same, jnp.concatenate([one, two, three], axis=1), NN, preferred_element_type=F32
        )
        sums[pl.ds(j, 64, stride=8), :] = added[:, 0:128] + (added[:, 128:256] + added[:, 256:384])
    returned = [
        copy(six(sums, place[1] * GZ + place[2]), six(got, 32 * core + chip), place)
        for _, _, place in plane
    ]
    got[pl.ds(pl.multiple_of((32 * core + chip) * 8, 8), 6), :] = sums[here_six, :]
    for c in returned:
        c.wait_recv()
    for k in range(2):
        for c in range(32):
            total[k, 6 * c : 6 * c + 6, :] = got[8 * (32 * k + c) : 8 * (32 * k + c) + 6, :]

    system[:, 0:COLS] = total[1]
    packed = total[0]
    one = packed[0:64, 0:64]
    below = packed[64:192, 0:64]
    middle = packed[64:128, 64:128]
    final = packed[128:192, 64:128]
    corner = packed[0:64, 64:128]
    blank = jnp.zeros((64, 64), F32)
    system[0:64, COLS : COLS + 256] = jnp.concatenate([one, below.T, blank], axis=1)
    system[64:192, COLS : COLS + 256] = jnp.concatenate(
        [
            below,
            jnp.concatenate([middle, final], axis=0),
            jnp.concatenate([final.T, corner], axis=0),
            jnp.zeros((128, 64), F32),
        ],
        axis=1,
    )
    lanes = lax.broadcasted_iota(jnp.int32, (NCON, 128), 1)
    down = lax.broadcasted_iota(jnp.int32, (NCON, 128), 0)
    tall_lane = lax.broadcasted_iota(jnp.int32, (COARSE, 128), 1)
    tall_row = lax.broadcasted_iota(jnp.int32, (COARSE, 128), 0)

    def placed(block, offset):
        parts = []
        if offset:
            parts.append(jnp.zeros((offset, block.shape[1]), block.dtype))
        parts.append(block)
        if offset + NCON < 128:
            parts.append(jnp.zeros((128 - NCON - offset, block.shape[1]), block.dtype))
        return jnp.concatenate(parts, axis=0)

    for k in range(FACES):
        rows = slice(k * NCON, (k + 1) * NCON)
        live = slice(0, COLS if k == FACES - 1 else 384)
        tile = slice(COLS + 128 * (k // 4), COLS + 128 * (k // 4) + 128)
        place = (k % 4) * NCON
        unit = (place + NCON) % 128
        in_unit = (lanes >= unit) & (lanes < unit + NCON)
        in_place = (lanes >= place) & (lanes < place + NCON)
        block = jnp.where(in_place, system[rows, tile], 0.0)
        block = jnp.where(lanes == down + unit, 1.0, block)
        slabs = [block[8 * v : 8 * v + 8] for v in range(4)]
        eliminate(
            [slabs],
            lambda slab, c, place=place: jnp.broadcast_to(
                slab[:, place + c : place + c + 1], slab.shape
            ),
            16,
            True,
        )
        pivot_inverse = jnp.where(in_unit, jnp.concatenate(slabs, axis=0), 0.0)
        scaled = product(
            split(pivot_inverse), [placed(part, unit) for part in split(system[rows, live])]
        )
        column = split(
            jnp.where(
                (tall_lane >= place) & (tall_lane < place + NCON), system[:, tile], 0.0
            )
        )
        scaled_parts = [placed(part, place) for part in split(scaled)]
        system[rows, live] = scaled

        def clear(low_row, high_row):
            if low_row < high_row:
                update = product([part[low_row:high_row] for part in column], scaled_parts)
                system[low_row:high_row, live] = system[low_row:high_row, live] - update

        clear((k + 1) * NCON, min((k + 2) * NCON, COARSE))
        clear((k + 2) * NCON, COARSE)
        clear(0, k * NCON)
    answer[...] = system[:, 0:COLS].reshape(FACES, NCON, COLS)
    answers = [
        copy(answer.at[f], partner_answer.at[f ^ 1], across(f)) for f in range(FACES)
    ]
    for f in (2, 3, 4, 5, 0, 1):
        answers[f ^ 1].wait_recv()
        both = jnp.concatenate([answer[f], partner_answer[f]], axis=0)
        correction[f * FACE : (f + 1) * FACE, :] = product(
            (mixed_high[f], mixed_low[f]), split(both)
        )
    for a in range(3):
        for c in (faces[a], starts[a], returns[a], mix_copies[a]):
            c.wait_send()
    for c in scattered + returned + answers:
        c.wait_send()


def array(*shape):
    return jax.ShapeDtypeStruct(shape, F32)


def remote(collective_id):
    return pltpu.CompilerParams(collective_id=collective_id, has_side_effects=True)


DMA = pltpu.SemaphoreType.DMA


def per_device(schur, start_block, resid, group_of):
    matrix = schur[0, 0, 0]
    pairs = (3, FACE, FACE)
    copies = 12 + 2 * 63 + 6
    correction = pl.pallas_call(
        main_kernel,
        out_shape=array(ORDER, COLS),
        in_specs=[VMEM] + [ANY] * 3,
        out_specs=VMEM,
        scratch_shapes=[
            pltpu.VMEM(pairs, F32),
            pltpu.VMEM((3, FACE + 8, FACE // 2), F32),
            pltpu.VMEM((3, FACE + 8, FACE // 2), F32),
            pltpu.VMEM((ORDER, ORDER), F32),
            pltpu.VMEM((ORDER, ORDER), BF16),
            pltpu.VMEM((ORDER, ORDER), BF16),
            pltpu.VMEM(pairs, F32),
            pltpu.VMEM(pairs, BF16),
            pltpu.VMEM(pairs, BF16),
            pltpu.VMEM(pairs, BF16),
            pltpu.VMEM(pairs, BF16),
            pltpu.VMEM((FACES, NCON, FACE), F32),
            pltpu.VMEM((3, NCON, FACE), F32),
            pltpu.VMEM((ORDER, COLS), F32),
            pltpu.VMEM((FACES + 3, NCON, FACE), F32),
            pltpu.VMEM((COARSE, ORDER), BF16),
            pltpu.VMEM((COARSE, ORDER), BF16),
            pltpu.VMEM((COARSE, ORDER), BF16),
            pltpu.VMEM((COARSE, ORDER), BF16),
            pltpu.VMEM((2, COARSE, COLS), F32),
            pltpu.VMEM((FACES + 3, 2 * NCON, FACE), F32),
            pltpu.VMEM((FACES, FACE, 2 * NCON), BF16),
            pltpu.VMEM((FACES, FACE, 2 * NCON), BF16),
            pltpu.VMEM((512, COLS), F32),
            pltpu.VMEM((512, COLS), F32),
            pltpu.VMEM((512, COLS), F32),
            pltpu.VMEM((512, COLS), F32),
            pltpu.VMEM((2, COARSE, COLS), F32),
            pltpu.VMEM((COARSE, 384), F32),
            pltpu.VMEM((FACES, NCON, COLS), F32),
            pltpu.VMEM((FACES, NCON, COLS), F32),
            DMA((copies,)),
            DMA((copies,)),
            DMA((11,)),
            pltpu.SemaphoreType.REGULAR,
        ],
        compiler_params=remote(0),
        name="main",
    )(group_of[None], matrix, jnp.swapaxes(start_block[0, 0, 0], 1, 2), resid[0, 0, 0])
    return correction[None, None, None]


def solution(mesh):
    in_specs = (
        P("gx", "gy", "gz", None, None),
        P("gx", "gy", "gz", None, None, None),
        P("gx", "gy", "gz", None, None),
        P(),
    )
    out_specs = P("gx", "gy", "gz", None, None)
    return jax.shard_map(
        per_device, mesh=mesh, in_specs=in_specs, out_specs=out_specs, check_vma=False
    )
```
